32 devices in a mesh: groups: 2 (over x), rows: 2 (over core), cols: 8 (over z, y).
Axes of the slice: x: 2, y: 2, z: 4, core: 2. Of those that a mesh axis runs over, the one named last changes fastest.
Arguments:
- feats: bfloat16 [16, 256, 256], P(('groups', 'rows'), 'cols'), parts along dimension 0, may hold values from -6 to 6
- w_in: bfloat16 [256, 512], replicated, may hold values from -0.375 to 0.375
- conv_w: float32 [9, 256], replicated, may hold values from -2 to 2
- conv_b: float32 [256], replicated, may hold values from -3 to 3
- w_proj: bfloat16 [4, 256, 144], replicated, may hold values from -0.375 to 0.375
- dt_bias: float32 [4, 16], replicated, may hold values from -4 to 1
- a_rate: float32 [4, 16], replicated, may hold values from 0.0001953125 to 0.1
- d_skip: float32 [4, 16], replicated, may hold values from 0.5 to 1.5
- norm_gain: float32 [256], replicated, may hold values from 0.1 to 1.9
- w_out: bfloat16 [256, 256], replicated, may hold values from -0.375 to 0.375
Outputs:
- mixed: bfloat16 [16, 256, 256], P(('groups', 'rows'), 'cols'), parts along dimension 0
The draws below stay inside these ranges and needn't reach their ends.
There are 2 independent parts, one for each index of `groups`. The reference program is written for one: setup_inputs(seed, part) draws one part's arguments, and reference() takes and returns one part's arrays. A program takes and returns all parts, laid end to end along the dimension named above; an argument that names none is the same for every part. Nothing has to cross between parts.
All inputs are finite; a program needn't handle non-finite values.
Results may differ from the reference program's by a relative error of at most 0.0097.
Values may be sent and summed in bfloat16 or wider, within the bound.
No kernel may reach another device: no remote copies, remote signals or barrier semaphores. Data moves between devices by JAX's collectives and lax.ppermute only.
A program may use at most 128 MiB of HBM per device.

```python
import math
import jax
import jax.numpy as jnp
from jax import lax

D = 256
NH = 16
NS = 64
TH = 4
TW = 32
H = 8
W = 256


def shard_levels(own_key, shape, shards, least, high):
    level, own = 1.0, jax.random.fold_in(own_key, 6)
    for dim, shards_of in shards:
        steps = jnp.exp(jax.random.uniform(jax.random.fold_in(own, dim), (shards_of,), jnp.float32, least / len(shards), high / len(shards)))
        level = level * jnp.repeat(steps, shape[dim] // shards_of).reshape([-1 if axis == dim else 1 for axis in range(len(shape))])
    return level


def gaussian(rng, extent, spread, reach, split=(), held_as=jnp.bfloat16):
    values = jax.random.normal(rng, extent, jnp.float32) * spread
    if len(split) > 0:
        values = shard_levels(rng, extent, split, -0.22, 0.18) * values
    return jnp.clip(values, min=-reach, max=reach).astype(held_as)


def setup_inputs(seed: int = 0, part: int = 0) -> dict:
    splits = jax.random.split(jax.random.key(seed), 11)
    part_keys = jax.random.split(jax.random.fold_in(splits[10], part), 11)
    feats = gaussian(part_keys[0], (H, W, D), 1.0, 6.0, ((0, 2), (1, 8)))
    w_in = gaussian(splits[1], (D, 2 * D), D ** -0.5, 0.375)
    conv_w = gaussian(splits[2], (9, D), 9 ** -0.5, 2.0, (), jnp.float32)
    conv_b = gaussian(splits[3], (D,), 0.5, 3.0, (), jnp.float32)
    w_proj = gaussian(splits[4], (4, D, NH + 2 * NS), D ** -0.5, 0.375)
    dt_bias = jnp.clip(jax.random.uniform(splits[5], (4, NH), jnp.float32, -4.0, 1.0), -4.0, 1.0)
    a_rate = jnp.clip(jnp.exp(jax.random.uniform(splits[6], (4, NH), jnp.float32, math.log(0.0001953125), math.log(0.1))), 0.0001953125, 0.1)
    d_skip = jnp.clip(jax.random.uniform(splits[7], (4, NH), jnp.float32, 0.5, 1.5), 0.5, 1.5)
    norm_gain = jnp.clip(1.0 + 0.18 * jax.random.normal(splits[8], (D,), jnp.float32), 0.1, 1.9)
    w_out = gaussian(splits[9], (D, D), D ** -0.5, 0.375)
    return {"feats": feats, "w_in": w_in, "conv_w": conv_w, "conv_b": conv_b, "w_proj": w_proj, "dt_bias": dt_bias, "a_rate": a_rate, "d_skip": d_skip, "norm_gain": norm_gain, "w_out": w_out}


norm_eps = 1e-05

def block_terms(inputs, step_sizes, write_vec, read_vec, rates, skips):
    seq_count, length, features = inputs.shape
    head_count = rates.shape[0]
    head_size = features // head_count
    cumul = jnp.cumsum(-step_sizes * rates, axis=1)
    scores = jnp.einsum('rtn,rsn->rts', read_vec.astype(jnp.float32), write_vec.astype(jnp.float32))
    places = jnp.arange(length)
    lower = places[:, None] >= places[None, :]
    cum_heads = jnp.swapaxes(cumul, 1, 2)
    gaps = cum_heads[:, :, :, None] - cum_heads[:, :, None, :]
    decays = jnp.where(lower, jnp.exp(jnp.minimum(gaps, 0.0)), 0.0)
    steps_heads = jnp.swapaxes(step_sizes, 1, 2)
    weights = (scores[:, None, :, :] * decays * steps_heads[:, :, None, :]).astype(jnp.bfloat16)
    per_head = inputs.reshape(seq_count, length, head_count, head_size)
    within = jnp.einsum('rhts,rshp->rthp', weights.astype(jnp.float32), per_head.astype(jnp.float32))
    within = within + skips[:, None] * per_head.astype(jnp.float32)
    to_end = jnp.exp(cumul[:, -1:, :] - cumul) * step_sizes
    scaled = (per_head.astype(jnp.float32) * to_end[..., None]).astype(jnp.bfloat16)
    states = jnp.einsum('rsn,rshp->rnhp', write_vec.astype(jnp.float32), scaled.astype(jnp.float32))
    nstate = write_vec.shape[2]
    return (within.reshape(seq_count, length, features), states.reshape(seq_count, nstate, features), jnp.exp(cumul[:, -1, :]), cumul)

def correction(read_vec, cumul, carried):
    seq_count, length, nstate = read_vec.shape
    features = carried.shape[-1]
    head_count = cumul.shape[-1]
    reads = jnp.einsum('rtn,rnd->rtd', read_vec.astype(jnp.float32), carried, precision=lax.Precision.HIGHEST)
    reads = reads.reshape(seq_count, length, head_count, features // head_count) * jnp.exp(cumul)[..., None]
    return reads.reshape(seq_count, length, features)

def advance_state(carried, decays, added):
    seq_count, nstate, features = carried.shape
    head_count = decays.shape[-1]
    kept = carried.reshape(seq_count, nstate, head_count, features // head_count) * decays[:, None, :, None]
    return kept.reshape(seq_count, nstate, features) + added

def run_blocks(inputs, step_sizes, write_vec, read_vec, rates, skips, block):
    seq_count, length, features = inputs.shape
    nblocks = length // block

    def to_blocks(array):
        return jnp.swapaxes(array.reshape((seq_count, nblocks, block) + array.shape[2:]), 0, 1)

    def advance(carried, pieces):
        within, added, decays, cumul = block_terms(pieces[0], pieces[1], pieces[2], pieces[3], rates, skips)
        results = within + correction(pieces[3], cumul, carried)
        return (advance_state(carried, decays, added), results)
    initial = jnp.zeros((seq_count, write_vec.shape[2], features), jnp.float32)
    _, results = lax.scan(advance, initial, (to_blocks(inputs), to_blocks(step_sizes), to_blocks(write_vec), to_blocks(read_vec)))
    return jnp.swapaxes(results, 0, 1).reshape(seq_count, length, features)

def run_grouped(inputs, step_sizes, write_vec, read_vec, rates, skips, block):
    seq_count = inputs.shape[0]
    group = math.gcd(seq_count, 256)

    def split_rows(array):
        return array.reshape((seq_count // group, group) + array.shape[1:])

    def one_group(pieces):
        return run_blocks(pieces[0], pieces[1], pieces[2], pieces[3], rates, skips, block)
    results = lax.map(one_group, (split_rows(inputs), split_rows(step_sizes), split_rows(write_vec), split_rows(read_vec)))
    return results.reshape(inputs.shape)

def direction_inputs(seqs, weight, bias, head_count):
    seq_count, length, features = seqs.shape
    projected = jnp.dot(seqs.reshape(-1, features), weight, preferred_element_type=jnp.float32)
    projected = projected.reshape(seq_count, length, -1)
    nstate = (projected.shape[-1] - head_count) // 2
    step_sizes = jax.nn.softplus(projected[..., :head_count] + bias)
    write_vec = projected[..., head_count:head_count + nstate].astype(jnp.bfloat16)
    read_vec = projected[..., head_count + nstate:].astype(jnp.bfloat16)
    return (step_sizes, write_vec, read_vec)

def direction(seqs, weight, bias, rates, skips, block, backward):
    if backward:
        seqs = jnp.flip(seqs, 1)
    step_sizes, write_vec, read_vec = direction_inputs(seqs, weight, bias, rates.shape[0])
    results = run_grouped(seqs, step_sizes, write_vec, read_vec, rates, skips, block)
    if backward:
        results = jnp.flip(results, 1)
    return results

def reference(feats, w_in, conv_w, conv_b, w_proj, dt_bias, a_rate, d_skip, norm_gain, w_out):
    height, breadth, features = feats.shape
    both = jnp.dot(feats.reshape(-1, features), w_in, preferred_element_type=jnp.float32)
    both = both.reshape(height, breadth, 2 * features)
    pre_conv = both[..., :features].astype(jnp.bfloat16)
    gate_in = both[..., features:]
    padded = jnp.pad(pre_conv, ((1, 1), (1, 1), (0, 0))).astype(jnp.float32)
    conv_sum = conv_b + jnp.zeros((height, breadth, features), jnp.float32)
    for offset in range(9):
        top = offset // 3
        left = offset % 3
        conv_sum = conv_sum + conv_w[offset] * padded[top:top + height, left:left + breadth]
    mixed_in = jax.nn.silu(conv_sum).astype(jnp.bfloat16)
    across = direction(mixed_in, w_proj[0], dt_bias[0], a_rate[0], d_skip[0], TW, False)
    across = across + direction(mixed_in, w_proj[1], dt_bias[1], a_rate[1], d_skip[1], TW, True)
    columns = jnp.swapaxes(mixed_in, 0, 1)
    down = direction(columns, w_proj[2], dt_bias[2], a_rate[2], d_skip[2], TH, False)
    down = down + direction(columns, w_proj[3], dt_bias[3], a_rate[3], d_skip[3], TH, True)
    vertical = jnp.swapaxes(down, 0, 1).astype(jnp.bfloat16)
    combined = across + vertical.astype(jnp.float32)
    centre = combined - lax.optimization_barrier(jnp.mean(combined, axis=-1, keepdims=True))
    normed = centre * lax.rsqrt(lax.optimization_barrier(jnp.mean(centre * centre, axis=-1, keepdims=True)) + norm_eps) * norm_gain
    gated = (normed * jax.nn.silu(gate_in)).astype(jnp.bfloat16)
    output = jnp.dot(gated.reshape(-1, features), w_out, preferred_element_type=jnp.float32)
    return output.reshape(height, breadth, features).astype(jnp.bfloat16)
```

```python
import functools

import jax
import jax.numpy as jnp
from jax import lax
from jax.experimental import pallas as pl
from jax.experimental.pallas import tpu as pltpu
from jax.sharding import PartitionSpec as P

norm_eps = 1e-05
f32, bf16 = jnp.float32, jnp.bfloat16
TH, TW, D, NH, NS = 4, 32, 256, 16, 64
HALO = 176


def dot(a, b):
    return jnp.dot(a, b, preferred_element_type=f32)


def dot_t(a, b):
    return lax.dot_general(a, b, (((1,), (1,)), ((), ())), preferred_element_type=f32)


def split(a):
    high = a.astype(bf16)
    return high, (a - high.astype(f32)).astype(bf16)


def dot_wide(a, mask):
    high, low = split(a)
    return dot(high, mask) + dot(low, mask)


def wide_dot(mask, b):
    high, low = split(b)
    return dot(mask, high) + dot(mask, low)


def softplus(x):
    return jnp.maximum(x, 0.0) + jnp.log1p(jnp.exp(-jnp.abs(x)))


def silu(x):
    return x * jax.nn.sigmoid(x)


def iotas(rows, lanes):
    return (
        lax.broadcasted_iota(jnp.int32, (rows, lanes), 0),
        lax.broadcasted_iota(jnp.int32, (rows, lanes), 1),
    )


def ones_where(mask):
    return jnp.where(mask, 1.0, 0.0).astype(bf16)


def at(g, j):
    start = g * (8 * TW) + TW * j
    return pl.ds(start if isinstance(start, int) else pl.multiple_of(start, TW), TW)


def each(count, body):
    if count == 1:
        body(0)
    else:
        lax.fori_loop(0, count, lambda i, carry: (body(i), carry)[1], 0)


def kernel(nb, gathered, place, *refs):
    count = 1 if gathered else nb
    blocks, refs = refs[:count], refs[count:]
    own_block, far, w_in, conv_w, conv_b, w_proj, dt_bias, a_rate, d_skip, gain, w_out, out = refs[:12]
    pre, strip, mixed, la_all, dt_all, totals, writes, scaled = refs[12:]
    row, col = place[0], place[1]
    lower = row == 1
    ng = nb // 8
    w_x = w_in[:, :D]

    def pre_conv(tokens):
        return dot(tokens, w_x).astype(bf16).astype(f32)

    pre[:, 0:8, :] = jnp.zeros((5, 8, D), f32)
    pre[:, 8 + nb * TW :, :] = jnp.zeros((5, 8, D), f32)

    def place_block(tokens, position):
        rows = pre_conv(tokens)
        base = pl.multiple_of(position * TW + 8, 8)
        for q in range(5):
            pre[q, pl.ds(base, TW), :] = rows[q * TW : (q + 1) * TW]

    if gathered:
        each(nb, lambda j: place_block(blocks[0][j, 0:160, :], j))
        left = blocks[0][jnp.maximum(col - 1, 0), 160:176, :]
        right = blocks[0][jnp.minimum(col + 1, nb - 1), 160:176, :]
    else:
        for step in range(nb):
            place_block(blocks[step][0:160, :], lax.rem(col - step + nb, nb))
        left, right = blocks[1][160:176, :], blocks[nb - 1][160:176, :]
    left = pre_conv(left) * jnp.where(col > 0, 1.0, 0.0)
    right = pre_conv(right) * jnp.where(col < nb - 1, 1.0, 0.0)
    far_pre = pre_conv(far[...])
    for i in range(3):
        strip[i, 8:40, :] = far_pre[i * TW : (i + 1) * TW]
        strip[i, 7:8, :] = left[8 + i : 9 + i]
        strip[i, 40:41, :] = right[i : i + 1]
    window = pl.multiple_of(col * TW, 32)
    for q in range(5):
        strip[3 + q] = pre[q, pl.ds(window, 48), :]

    taps = [
        [
            jnp.where(lower, conv_w[3 * a + b : 3 * a + b + 1, :], conv_w[3 * (2 - a) + b : 3 * (2 - a) + b + 1, :])
            for b in range(3)
        ]
        for a in range(3)
    ]
    bias = conv_b[...]

    def filtered(ref, count, q, base):
        total = jnp.broadcast_to(bias, (TW, D))
        for a in range(3):
            if 0 <= q + a - 1 < count:
                if not isinstance(base, int):
                    cells = ref[q + a - 1, pl.ds(pl.multiple_of(base - 8, 8), TW + 16), :]
                for b in range(3):
                    if isinstance(base, int):
                        value = ref[q + a - 1, base + b - 1 : base + b - 1 + TW, :]
                    else:
                        value = cells[7 + b : 7 + b + TW]
                    total = total + taps[a][b] * value
        return silu(total).astype(bf16)

    strip_mixed = [filtered(strip, 8, q, 8) for q in range(8)]
    own = jnp.concatenate(strip_mixed[4:], axis=0)
    column_tokens = jnp.concatenate(strip_mixed, axis=0)

    head_lane = ones_where(iotas(NH, 128)[1] % NH == iotas(NH, 128)[0])
    expand = ones_where(iotas(NH, D)[1] // NH == iotas(NH, D)[0])
    tok_r, tok_c = iotas(128, 128)
    same_row = tok_r // TW == tok_c // TW
    after = ones_where(same_row & (tok_c > tok_r))
    before = ones_where(same_row & (tok_c < tok_r))
    upto = ones_where(same_row & (tok_c <= tok_r))
    onward = ones_where(same_row & (tok_c >= tok_r))
    row_ones = ones_where(same_row)

    lane = lax.broadcasted_iota(jnp.int32, (1, 128), 1)
    bias_2 = dot_wide(dt_bias[0:2, :], head_lane)
    rate_2 = dot_wide(a_rate[0:2, :], head_lane)
    w_step = [dot(w_proj[k, :, 0:NH], head_lane) for k in range(2)]
    w_write = jnp.concatenate([w_proj[0, :, NH : NH + NS], w_proj[1, :, NH : NH + NS]], axis=1)

    def first_pass(g):
        group = lane // NH + g * 8
        is_left = group < col
        w_both = jnp.concatenate([jnp.where(is_left, w_step[0], w_step[1]).astype(bf16), w_write], axis=1)
        raw = jnp.zeros((128, 128), f32)
        for j in range(8):
            base = g * (8 * TW) + (8 + TW * j)
            for q in range(1, 5):
                mixed[g * 8 + j, (q - 1) * TW : q * TW, :] = filtered(pre, 5, q, base)
            result = dot(mixed[g * 8 + j], w_both)
            raw = jnp.where(lane // NH == j, result[:, :128], raw)
            block = g * 8 + j
            keep = jnp.where(lane < NS, jnp.where(block < col, 1.0, 0.0), jnp.where(block > col, 1.0, 0.0))
            vectors = (result[:, 128:] * keep).astype(bf16)
            for q in range(4):
                writes[q, at(g, j), :] = vectors[q * TW : (q + 1) * TW]
        steps = softplus(raw + jnp.where(is_left, bias_2[0:1], bias_2[1:2]))
        steps = jnp.where(group == col, 0.0, steps)
        logs = -steps * jnp.where(is_left, rate_2[0:1], rate_2[1:2])
        dt_all[g] = steps
        la_all[g] = logs
        totals[g] = wide_dot(row_ones, logs)

    each(ng, first_pass)

    both_ways = jnp.concatenate([after, before], axis=1)

    def second_pass(g):
        group = lane // NH + g * 8
        logs = la_all[g]
        stacked = jnp.concatenate([jnp.where(group < col, logs, 0.0), jnp.where(group > col, logs, 0.0)], axis=0)
        reach = wide_dot(both_ways, stacked)

        def add_group(other, total):
            source, target = other * 8 + tok_r // NH, g * 8 + tok_c // NH
            nearer = ((source > target) & (source < col)) | ((source < target) & (source > col))
            nearer = nearer & (tok_r % NH == tok_c % NH)
            return total + dot_wide(totals[other], ones_where(nearer))

        if ng == 1:
            reach = add_group(0, reach)
        else:
            reach = lax.fori_loop(0, ng, add_group, reach)
        weight = jnp.concatenate(split(jnp.exp(reach) * dt_all[g]), axis=1)
        expand_r, expand_c = iotas(256, D)
        for j in range(8):
            pick = ones_where((expand_r % 128) == j * NH + expand_c // NH)
            factor = dot(weight, pick)
            values = (mixed[g * 8 + j].astype(f32) * factor).astype(bf16)
            for q in range(4):
                scaled[q, at(g, j), :] = values[q * TW : (q + 1) * TW]

    each(ng, second_pass)

    projected = [dot(own, w_proj[k]) for k in range(2)]
    steps = [softplus(projected[k][:, :NH] + dt_bias[k : k + 1, :]) for k in range(2)]
    logs = [-steps[k] * a_rate[k : k + 1, :] for k in range(2)]
    write = [projected[k][:, NH : NH + NS].astype(bf16) for k in range(2)]
    read = [projected[k][:, NH + NS :].astype(bf16) for k in range(2)]
    from_edge = [
        dot_wide(jnp.exp(wide_dot(mask, logs[k])), expand) for k, mask in enumerate((upto, onward))
    ]
    pair_r, pair_c = iotas(NH, NH * TW)
    spread = ones_where(pair_c // TW == pair_r)
    inner_r, inner_c = iotas(128, NH * TW)
    inner_u, inner_s = inner_r % TW, inner_c % TW
    parts = []
    for k, keep in enumerate((inner_u > inner_s, inner_u < inner_s)):
        for part in split(logs[k]):
            parts.append(jnp.where(keep, dot(part, spread), 0.0).astype(bf16))
    step_parts = [jnp.where(inner_u == inner_s, dot_wide(steps[k], spread), 0.0) for k in range(2)]
    time_r, time_c = iotas(TW, TW)
    first, second = ones_where(time_c <= time_r), ones_where(time_c >= time_r)
    walk = jnp.concatenate([first, first, second, second], axis=1)
    local_t, local_s = iotas(TW, NH * TW)
    local_s = local_s % TW
    feature = lax.broadcasted_iota(jnp.int32, (TW, D), 1) // NH
    zeros = jnp.zeros((TW, NS), bf16)
    across = []
    for q in range(4):
        rows = slice(q * TW, (q + 1) * TW)
        gaps = dot(walk, jnp.concatenate([part[rows] for part in parts], axis=0))
        weights = jnp.zeros((TW, NH * TW), f32)
        for k, keep in enumerate((local_s <= local_t, local_s >= local_t)):
            scores = dot_t(read[k][rows], jnp.concatenate([write[k][rows]] * NH, axis=0))
            step_row = jnp.sum(step_parts[k][rows], axis=0, keepdims=True)
            weights = weights + jnp.where(keep, scores * step_row, 0.0)
        weights = (weights * jnp.exp(gaps)).astype(bf16)
        values = own[rows]
        spread_values = jnp.concatenate(
            [jnp.where(feature == h, values, jnp.zeros_like(values)) for h in range(NH)], axis=0
        )
        result = dot(weights, spread_values)
        state = lax.dot_general(writes[q], scaled[q], (((0,), (0,)), ((), ())), preferred_element_type=f32)
        reads = jnp.concatenate(
            [
                jnp.concatenate([read[0][rows], zeros], axis=1),
                jnp.concatenate([zeros, read[1][rows]], axis=1),
            ],
            axis=0,
        )
        entered = wide_dot(reads, state)
        result = result + entered[:TW] * from_edge[0][rows] + entered[TW:] * from_edge[1][rows]
        across.append(result)
    across = jnp.concatenate(across, axis=0)

    k_in = jnp.where(lower, 2, 3)
    k_out = jnp.where(lower, 3, 2)

    def pick_row(ref, k):
        return jnp.where(k == 2, ref[2:3, :], ref[3:4, :])

    project_in = dot(column_tokens, w_proj[k_in])
    project_out = dot(own, w_proj[k_out])
    steps_in = softplus(project_in[:, :NH] + pick_row(dt_bias, k_in))
    steps_out = softplus(project_out[:, :NH] + pick_row(dt_bias, k_out))
    logs_in = -steps_in * pick_row(a_rate, k_in)
    logs_out = -steps_out * pick_row(a_rate, k_out)
    write_in = project_in[:, NH : NH + NS].astype(bf16)
    write_out = project_out[:, NH : NH + NS].astype(bf16)
    read_in = project_in[128:, NH + NS :].astype(bf16)
    read_out = project_out[:, NH + NS :].astype(bf16)
    t_r, s_c = iotas(128, 256)
    same_col = (t_r % TW) == (s_c % TW)
    meet_in = ones_where(same_col)
    walk_in = ones_where(same_col & (s_c // TW <= t_r // TW + 4))
    meet_out = ones_where(tok_r % TW == tok_c % TW)
    walk_out = ones_where((tok_r % TW == tok_c % TW) & (tok_c >= tok_r))
    source_r, source_c = iotas(256, 128)
    source_u, source_s = source_r // TW, source_c // NH
    select = ones_where(source_u == source_s)
    scores_in = dot_wide(jnp.where(same_col, dot_t(read_in, write_in), 0.0), select)
    same_out = tok_r % TW == tok_c % TW
    scores_out = dot_wide(jnp.where(same_out, dot_t(read_out, write_out), 0.0), select[128:])
    out_u = tok_r // TW + 4
    out_s = tok_c // NH
    gap = jnp.zeros((128, 128), f32)
    for part in split(logs_in):
        gap = gap + dot(walk_in, jnp.where(source_u > source_s, dot(part, head_lane), 0.0).astype(bf16))
    for part in split(logs_out):
        gap = gap + dot(walk_out, jnp.where(out_u < out_s, dot(part, head_lane), 0.0).astype(bf16))
    lane_in = jnp.zeros((128, 128), f32)
    for part in split(steps_in):
        lane_in = lane_in + dot(meet_in, jnp.where(source_u == source_s, dot(part, head_lane), 0.0).astype(bf16))
    lane_out = jnp.zeros((128, 128), f32)
    for part in split(steps_out):
        lane_out = lane_out + dot(meet_out, jnp.where(out_u == out_s, dot(part, head_lane), 0.0).astype(bf16))
    weights = jnp.where(out_s <= out_u, scores_in * lane_in, 0.0) + jnp.where(out_s >= out_u, scores_out * lane_out, 0.0)
    weights = (weights * jnp.exp(gap)).astype(bf16)
    skips = dot_wide(d_skip[...], expand)
    own_wide = own.astype(f32)
    pick_r, pick_c = iotas(128, D)
    vertical = (skips[2:3] + skips[3:4]) * own_wide
    for s in range(8):
        factor = dot(weights, ones_where(pick_r == s * NH + pick_c // NH))
        values = strip_mixed[s].astype(f32)
        vertical = vertical + factor * jnp.concatenate([values] * 4, axis=0)
    combined = across + (skips[0:1] + skips[1:2]) * own_wide + vertical.astype(bf16).astype(f32)

    centre = combined - jnp.mean(combined, axis=-1, keepdims=True)
    normed = centre * lax.rsqrt(jnp.mean(centre * centre, axis=-1, keepdims=True) + norm_eps) * gain[...]
    gate_in = dot(own_block[TW:160, :], w_in[:, D:])
    gated = (normed * silu(gate_in)).astype(bf16)
    result = dot(gated, w_out[...]).astype(bf16)
    for i in range(4):
        out[jnp.where(lower, i, 3 - i)] = result[i * TW : (i + 1) * TW]


def shards(feats, w_in, conv_w, conv_b, w_proj, dt_bias, a_rate, d_skip, norm_gain, w_out):
    nb = lax.axis_size("cols")
    row, col = lax.axis_index("rows"), lax.axis_index("cols")
    partner = lax.ppermute(feats, "rows", [(0, 1), (1, 0)])
    ordered = jnp.concatenate([partner, feats], axis=0)
    turned = jnp.concatenate([partner[::-1], feats[::-1]], axis=0)
    ordered = jnp.where(row == 1, ordered, turned)
    far = ordered[:3]
    pad = jnp.zeros((5, D), bf16)
    sent = jnp.concatenate([ordered[3:].reshape(160, D), far[:, 0], pad, far[:, TW - 1], pad], axis=0)
    if nb == 8:
        blocks = [sent]
        for step in range(1, nb):
            blocks.append(lax.ppermute(sent, "cols", [(i, (i + step) % nb) for i in range(nb)]))
    else:
        blocks = [lax.all_gather(sent, "cols")]
    operands = [
        *blocks,
        sent,
        far.reshape(96, D),
        w_in,
        conv_w,
        conv_b[None],
        w_proj,
        dt_bias,
        a_rate,
        d_skip,
        norm_gain[None],
        w_out,
    ]
    vmem = pl.BlockSpec(memory_space=pltpu.VMEM)
    return pl.pallas_call(
        functools.partial(kernel, nb, nb != 8),
        out_shape=jax.ShapeDtypeStruct((TH, TW, D), bf16),
        in_specs=[pl.BlockSpec(memory_space=pltpu.SMEM)] + [vmem] * len(operands),
        out_specs=vmem,
        scratch_shapes=[
            pltpu.VMEM((5, nb * TW + 16, D), f32),
            pltpu.VMEM((8, 48, D), f32),
            pltpu.VMEM((nb, 128, D), bf16),
            pltpu.VMEM((nb // 8, 128, 128), f32),
            pltpu.VMEM((nb // 8, 128, 128), f32),
            pltpu.VMEM((nb // 8, 128, 128), f32),
            pltpu.VMEM((4, nb * TW, 128), bf16),
            pltpu.VMEM((4, nb * TW, D), bf16),
        ],
        cost_estimate=pl.CostEstimate(flops=2_000_000_000, bytes_accessed=4_000_000, transcendentals=1_000_000),
    )(jnp.stack([row, col]).astype(jnp.int32), *operands)


def solution(mesh):
    in_specs = (P(("groups", "rows"), "cols", None), P(), P(), P(), P(), P(), P(), P(), P(), P())
    out_specs = P(("groups", "rows"), "cols", None)
    return jax.shard_map(shards, mesh=mesh, in_specs=in_specs, out_specs=out_specs, check_vma=False)
```

```python
import functools

import jax
import jax.numpy as jnp
from jax import lax
from jax.experimental import pallas as pl
from jax.experimental.pallas import tpu as pltpu
from jax.sharding import PartitionSpec as P

norm_eps = 1e-05
f32, bf16 = jnp.float32, jnp.bfloat16
TH, TW, D, NH, NS = 4, 32, 256, 16, 64
HALO = 176


def dot(a, b):
    return jnp.dot(a, b, preferred_element_type=f32)


def dot_t(a, b):
    return lax.dot_general(a, b, (((1,), (1,)), ((), ())), preferred_element_type=f32)


def split(a):
    high = a.astype(bf16)
    return high, (a - high.astype(f32)).astype(bf16)


def dot_wide(a, mask):
    high, low = split(a)
    return dot(high, mask) + dot(low, mask)


def wide_dot(mask, b):
    high, low = split(b)
    return dot(mask, high) + dot(mask, low)


def softplus(x):
    return jnp.maximum(x, 0.0) + jnp.log1p(jnp.exp(-jnp.abs(x)))


def silu(x):
    return x * jax.nn.sigmoid(x)


def iotas(rows, lanes):
    return (
        lax.broadcasted_iota(jnp.int32, (rows, lanes), 0),
        lax.broadcasted_iota(jnp.int32, (rows, lanes), 1),
    )


def ones_where(mask):
    return jnp.where(mask, 1.0, 0.0).astype(bf16)


def at(g, j):
    start = g * (8 * TW) + TW * j
    return pl.ds(start if isinstance(start, int) else pl.multiple_of(start, TW), TW)


def each(count, body):
    if count == 1:
        body(0)
    else:
        lax.fori_loop(0, count, lambda i, carry: (body(i), carry)[1], 0)


def load(feats, w_in, conv_w, conv_b, w_proj, dt_bias, a_rate, d_skip, gain, w_out, *refs):
    lower = lax.axis_index("rows") == 1
    sent, outs, sems = refs[0], refs[1:-1], refs[-1]
    copies = [
        pltpu.make_async_copy(
            feats.at[jnp.where(lower, i, 3 - i)], sent.at[pl.ds(TW * (i + 1), TW), :], sems.at[i]
        )
        for i in range(4)
    ]
    weights = (w_in, conv_w, conv_b, w_proj, dt_bias, a_rate, d_skip, gain, w_out)
    copies += [
        pltpu.make_async_copy(source, target, sems.at[4 + i])
        for i, (source, target) in enumerate(zip(weights, outs))
    ]
    for copy in copies:
        copy.start()
    for copy in copies:
        copy.wait()


def pack(loaded, partner, sent, far):
    lower = lax.axis_index("rows") == 1
    own = [loaded[TW * (i + 1) : TW * (i + 2), :] for i in range(4)]
    rows = [partner[jnp.where(lower, i, 3 - i)] for i in range(4)] + own
    for i in range(3, 8):
        sent[TW * (i - 3) : TW * (i - 2), :] = rows[i]
    for i in range(3):
        far[i * TW : (i + 1) * TW, :] = rows[i]
    wide = [part.astype(f32) for part in rows]
    edges = [part[:1] for part in wide] + [part[TW - 1 :] for part in wide]
    sent[160:HALO, :] = jnp.concatenate(edges, axis=0).astype(bf16)


def direction_taps(conv_w, lower):
    return [
        [
            jnp.where(lower, conv_w[3 * a + b : 3 * a + b + 1, :], conv_w[3 * (2 - a) + b : 3 * (2 - a) + b + 1, :])
            for b in range(3)
        ]
        for a in range(3)
    ]


def filtered(ref, count, q, base, taps, bias):
    total = jnp.broadcast_to(bias, (TW, D))
    for a in range(3):
        if 0 <= q + a - 1 < count:
            if not isinstance(base, int):
                cells = ref[q + a - 1, pl.ds(pl.multiple_of(base - 8, 8), TW + 16), :]
            for b in range(3):
                if isinstance(base, int):
                    value = ref[q + a - 1, base + b - 1 : base + b - 1 + TW, :]
                else:
                    value = cells[7 + b : 7 + b + TW]
                total = total + taps[a][b] * value
    return silu(total).astype(bf16)


def local(nb, count, sent, far, *refs):
    sides, refs = refs[:count], refs[count:]
    w_in, conv_w, conv_b, w_proj, dt_bias, a_rate, d_skip = refs[:7]
    base_out, gate_out, reads_out, edge_out, strip = refs[7:]
    row, col = lax.axis_index("rows"), lax.axis_index("cols")
    lower = row == 1
    w_x = w_in[:, :D]

    def pre_conv(tokens):
        return dot(tokens, w_x).astype(bf16).astype(f32)

    if count == 1:
        left = sides[0][jnp.maximum(col - 1, 0), 160:HALO, :]
        right = sides[0][jnp.minimum(col + 1, nb - 1), 160:HALO, :]
    else:
        near, further, furthest = (side[160:HALO, :] for side in sides)
        odd = lax.rem(col, 2) == 1
        left = jnp.where(odd, near, jnp.where(col == 4, furthest, further))
        right = jnp.where(odd, jnp.where(col == 3, furthest, further), near)
    left = pre_conv(left) * jnp.where(col > 0, 1.0, 0.0)
    right = pre_conv(right) * jnp.where(col < nb - 1, 1.0, 0.0)
    far_pre, own_pre = pre_conv(far[...]), pre_conv(sent[0:160, :])
    for i in range(8):
        strip[i, 8:40, :] = far_pre[i * TW : (i + 1) * TW] if i < 3 else own_pre[(i - 3) * TW : (i - 2) * TW]
        strip[i, 7:8, :] = left[8 + i : 9 + i]
        strip[i, 40:41, :] = right[i : i + 1]
    taps, bias = direction_taps(conv_w, lower), conv_b[...]
    strip_mixed = [filtered(strip, 8, q, 8, taps, bias) for q in range(8)]
    own = jnp.concatenate(strip_mixed[4:], axis=0)
    column_tokens = jnp.concatenate(strip_mixed, axis=0)
    gate_out[...] = silu(dot(sent[TW:160, :], w_in[:, D:]))

    head_lane = ones_where(iotas(NH, 128)[1] % NH == iotas(NH, 128)[0])
    expand = ones_where(iotas(NH, D)[1] // NH == iotas(NH, D)[0])
    tok_r, tok_c = iotas(128, 128)
    same_row = tok_r // TW == tok_c // TW
    upto = ones_where(same_row & (tok_c <= tok_r))
    onward = ones_where(same_row & (tok_c >= tok_r))

    projected = [dot_t(own, w_proj[k]) for k in range(2)]
    steps = [softplus(projected[k][:, :NH] + dt_bias[k : k + 1, :]) for k in range(2)]
    logs = [-steps[k] * a_rate[k : k + 1, :] for k in range(2)]
    write = [projected[k][:, NH : NH + NS].astype(bf16) for k in range(2)]
    read = [projected[k][:, NH + NS :].astype(bf16) for k in range(2)]
    from_edge = [
        dot_wide(jnp.exp(wide_dot(mask, logs[k])), expand) for k, mask in enumerate((upto, onward))
    ]
    edge_out[0], edge_out[1] = from_edge
    pair_r, pair_c = iotas(NH, NH * TW)
    spread = ones_where(pair_c // TW == pair_r)
    inner_r, inner_c = iotas(128, NH * TW)
    inner_u, inner_s = inner_r % TW, inner_c % TW
    parts = []
    for k, keep in enumerate((inner_u > inner_s, inner_u < inner_s)):
        for part in split(logs[k]):
            parts.append(jnp.where(keep, dot(part, spread), 0.0).astype(bf16))
    step_parts = [jnp.where(inner_u == inner_s, dot_wide(steps[k], spread), 0.0) for k in range(2)]
    time_r, time_c = iotas(TW, TW)
    first, second = ones_where(time_c <= time_r), ones_where(time_c >= time_r)
    walk = jnp.concatenate([first, first, second, second], axis=1)
    local_t, local_s = iotas(TW, NH * TW)
    local_s = local_s % TW
    feature = lax.broadcasted_iota(jnp.int32, (TW, D), 1) // NH
    zeros = jnp.zeros((TW, NS), bf16)
    across = []
    for q in range(4):
        rows = slice(q * TW, (q + 1) * TW)
        gaps = dot(walk, jnp.concatenate([part[rows] for part in parts], axis=0))
        weights = jnp.zeros((TW, NH * TW), f32)
        for k, keep in enumerate((local_s <= local_t, local_s >= local_t)):
            scores = dot_t(read[k][rows], jnp.concatenate([write[k][rows]] * NH, axis=0))
            step_row = jnp.sum(step_parts[k][rows], axis=0, keepdims=True)
            weights = weights + jnp.where(keep, scores * step_row, 0.0)
        weights = (weights * jnp.exp(gaps)).astype(bf16)
        values = own[rows]
        spread_values = jnp.concatenate(
            [jnp.where(feature == h, values, jnp.zeros_like(values)) for h in range(NH)], axis=0
        )
        result = dot(weights, spread_values)
        reads = jnp.concatenate(
            [
                jnp.concatenate([read[0][rows], zeros], axis=1),
                jnp.concatenate([zeros, read[1][rows]], axis=1),
            ],
            axis=0,
        )
        reads_out[q] = reads
        across.append(result)
    across = jnp.concatenate(across, axis=0)

    k_in = jnp.where(lower, 2, 3)
    k_out = jnp.where(lower, 3, 2)

    def pick_row(ref, k):
        return jnp.where(k == 2, ref[2:3, :], ref[3:4, :])

    project_in = dot_t(column_tokens, w_proj[k_in])
    project_out = dot_t(own, w_proj[k_out])
    steps_in = softplus(project_in[:, :NH] + pick_row(dt_bias, k_in))
    steps_out = softplus(project_out[:, :NH] + pick_row(dt_bias, k_out))
    logs_in = -steps_in * pick_row(a_rate, k_in)
    logs_out = -steps_out * pick_row(a_rate, k_out)
    write_in = project_in[:, NH : NH + NS].astype(bf16)
    write_out = project_out[:, NH : NH + NS].astype(bf16)
    read_in = project_in[128:, NH + NS :].astype(bf16)
    read_out = project_out[:, NH + NS :].astype(bf16)
    t_r, s_c = iotas(128, 256)
    same_col = (t_r % TW) == (s_c % TW)
    meet_in = ones_where(same_col)
    walk_in = ones_where(same_col & (s_c // TW <= t_r // TW + 4))
    meet_out = ones_where(tok_r % TW == tok_c % TW)
    walk_out = ones_where((tok_r % TW == tok_c % TW) & (tok_c >= tok_r))
    source_r, source_c = iotas(256, 128)
    source_u, source_s = source_r // TW, source_c // NH
    select = ones_where(source_u == source_s)
    scores_in = dot_wide(jnp.where(same_col, dot_t(read_in, write_in), 0.0), select)
    same_out = tok_r % TW == tok_c % TW
    scores_out = dot_wide(jnp.where(same_out, dot_t(read_out, write_out), 0.0), select[128:])
    out_u = tok_r // TW + 4
    out_s = tok_c // NH
    gap = jnp.zeros((128, 128), f32)
    for part in split(logs_in):
        gap = gap + dot(walk_in, jnp.where(source_u > source_s, dot(part, head_lane), 0.0).astype(bf16))
    for part in split(logs_out):
        gap = gap + dot(walk_out, jnp.where(out_u < out_s, dot(part, head_lane), 0.0).astype(bf16))
    lane_in = jnp.zeros((128, 128), f32)
    for part in split(steps_in):
        lane_in = lane_in + dot(meet_in, jnp.where(source_u == source_s, dot(part, head_lane), 0.0).astype(bf16))
    lane_out = jnp.zeros((128, 128), f32)
    for part in split(steps_out):
        lane_out = lane_out + dot(meet_out, jnp.where(out_u == out_s, dot(part, head_lane), 0.0).astype(bf16))
    weights = jnp.where(out_s <= out_u, scores_in * lane_in, 0.0) + jnp.where(out_s >= out_u, scores_out * lane_out, 0.0)
    weights = (weights * jnp.exp(gap)).astype(bf16)
    skips = dot_wide(d_skip[...], expand)
    own_wide = own.astype(f32)
    pick_r, pick_c = iotas(128, D)
    vertical = (skips[2:3] + skips[3:4]) * own_wide
    for s in range(8):
        factor = dot(weights, ones_where(pick_r == s * NH + pick_c // NH))
        values = strip_mixed[s].astype(f32)
        vertical = vertical + factor * jnp.concatenate([values] * 4, axis=0)
    base_out[...] = across + (skips[0:1] + skips[1:2]) * own_wide + vertical.astype(bf16).astype(f32)


def final(nb, gathered, *refs):
    count = 1 if gathered else nb
    blocks, refs = refs[:count], refs[count:]
    base_in, gate_in, reads_in, edge_in = refs[:4]
    w_in, conv_w, conv_b, w_proj, dt_bias, a_rate, gain, w_out, out = refs[4:13]
    pre, mixed, la_all, dt_all, totals, writes, scaled = refs[13:]
    row, col = lax.axis_index("rows"), lax.axis_index("cols")
    lower = row == 1
    ng = nb // 8
    w_x = w_in[:, :D]

    def pre_conv(tokens):
        return dot(tokens, w_x).astype(bf16).astype(f32)

    pre[:, 0:8, :] = jnp.zeros((5, 8, D), f32)
    pre[:, 8 + nb * TW :, :] = jnp.zeros((5, 8, D), f32)

    def place_block(tokens, position):
        rows = pre_conv(tokens)
        base = pl.multiple_of(position * TW + 8, 8)
        for q in range(5):
            pre[q, pl.ds(base, TW), :] = rows[q * TW : (q + 1) * TW]

    if gathered:
        each(nb, lambda j: place_block(blocks[0][j, 0:160, :], j))
    else:
        for step in range(nb):
            place_block(blocks[step][0:160, :], col ^ step)
    taps, bias = direction_taps(conv_w, lower), conv_b[...]

    head_lane = ones_where(iotas(NH, 128)[1] % NH == iotas(NH, 128)[0])
    tok_r, tok_c = iotas(128, 128)
    same_row = tok_r // TW == tok_c // TW
    after = ones_where(same_row & (tok_c > tok_r))
    before = ones_where(same_row & (tok_c < tok_r))
    row_ones = ones_where(same_row)
    lane = lax.broadcasted_iota(jnp.int32, (1, 128), 1)
    bias_2 = dot_wide(dt_bias[0:2, :], head_lane)
    rate_2 = dot_wide(a_rate[0:2, :], head_lane)

    def first_pass(g):
        group = lane // NH + g * 8
        is_left = group < col
        w_both = jnp.concatenate(
            [jnp.where(g * 8 + j < col, w_proj[0, 0:NH, :], w_proj[1, 0:NH, :]) for j in range(8)]
            + [w_proj[k, NH : NH + NS, :] for k in range(2)],
            axis=0,
        )
        raw = jnp.zeros((128, 128), f32)
        for j in range(8):
            base = g * (8 * TW) + (8 + TW * j)
            for q in range(1, 5):
                mixed[g * 8 + j, (q - 1) * TW : q * TW, :] = filtered(pre, 5, q, base, taps, bias)
            result = dot_t(mixed[g * 8 + j], w_both)
            raw = jnp.where(lane // NH == j, result[:, :128], raw)
            block = g * 8 + j
            keep = jnp.where(lane < NS, jnp.where(block < col, 1.0, 0.0), jnp.where(block > col, 1.0, 0.0))
            vectors = (result[:, 128:] * keep).astype(bf16)
            for q in range(4):
                writes[q, at(g, j), :] = vectors[q * TW : (q + 1) * TW]
        steps = softplus(raw + jnp.where(is_left, bias_2[0:1], bias_2[1:2]))
        steps = jnp.where(group == col, 0.0, steps)
        logs = -steps * jnp.where(is_left, rate_2[0:1], rate_2[1:2])
        dt_all[g] = steps
        la_all[g] = logs
        totals[g] = wide_dot(row_ones, logs)

    each(ng, first_pass)

    both_ways = jnp.concatenate([after, before], axis=1)

    def second_pass(g):
        group = lane // NH + g * 8
        logs = la_all[g]
        stacked = jnp.concatenate([jnp.where(group < col, logs, 0.0), jnp.where(group > col, logs, 0.0)], axis=0)
        reach = wide_dot(both_ways, stacked)

        def add_group(other, total):
            source, target = other * 8 + tok_r // NH, g * 8 + tok_c // NH
            nearer = ((source > target) & (source < col)) | ((source < target) & (source > col))
            nearer = nearer & (tok_r % NH == tok_c % NH)
            return total + dot_wide(totals[other], ones_where(nearer))

        if ng == 1:
            reach = add_group(0, reach)
        else:
            reach = lax.fori_loop(0, ng, add_group, reach)
        weight = jnp.concatenate(split(jnp.exp(reach) * dt_all[g]), axis=1)
        expand_r, expand_c = iotas(256, D)
        for j in range(8):
            pick = ones_where((expand_r % 128) == j * NH + expand_c // NH)
            factor = dot(weight, pick)
            values = (mixed[g * 8 + j].astype(f32) * factor).astype(bf16)
            for q in range(4):
                scaled[q, at(g, j), :] = values[q * TW : (q + 1) * TW]

    each(ng, second_pass)

    entered = []
    for q in range(4):
        rows = slice(q * TW, (q + 1) * TW)
        state = lax.dot_general(writes[q], scaled[q], (((0,), (0,)), ((), ())), preferred_element_type=f32)
        both = wide_dot(reads_in[q], state)
        entered.append(both[:TW] * edge_in[0, rows, :] + both[TW:] * edge_in[1, rows, :])
    combined = base_in[...] + jnp.concatenate(entered, axis=0)

    centre = combined - jnp.mean(combined, axis=-1, keepdims=True)
    normed = centre * lax.rsqrt(jnp.mean(centre * centre, axis=-1, keepdims=True) + norm_eps) * gain[...]
    gated = (normed * gate_in[...]).astype(bf16)
    result = dot(gated, w_out[...]).astype(bf16)
    for i in range(4):
        out[jnp.where(lower, i, 3 - i)] = result[i * TW : (i + 1) * TW]


def shards(feats, w_in, conv_w, conv_b, w_proj, dt_bias, a_rate, d_skip, norm_gain, w_out):
    nb = lax.axis_size("cols")
    direct = nb == 8
    vmem, hbm = pl.BlockSpec(memory_space=pltpu.VMEM), pl.BlockSpec(memory_space=pltpu.HBM)

    def shape(*dims, dtype=f32):
        return jax.ShapeDtypeStruct(dims, dtype)

    def limit(mib):
        return pltpu.CompilerParams(vmem_limit_bytes=mib << 20)

    partner = lax.ppermute(feats, "rows", [(0, 1), (1, 0)])
    params = [w_in, conv_w, conv_b[None], jnp.swapaxes(w_proj, 1, 2), dt_bias, a_rate, d_skip, norm_gain[None], w_out]
    loaded, *params = pl.pallas_call(
        load,
        out_shape=(shape(HALO, D, dtype=bf16), *[shape(*part.shape, dtype=part.dtype) for part in params]),
        in_specs=[hbm] * 10,
        out_specs=(vmem,) * 10,
        scratch_shapes=[pltpu.SemaphoreType.DMA((13,))],
        compiler_params=limit(8),
    )(*[pltpu.with_memory_space_constraint(part, pltpu.HBM) for part in (feats, *params)])
    w_in, conv_w, conv_b, w_proj, dt_bias, a_rate, d_skip, norm_gain, w_out = params
    sent, far = pl.pallas_call(
        pack,
        out_shape=(shape(HALO, D, dtype=bf16), shape(96, D, dtype=bf16)),
        in_specs=[vmem] * 2,
        out_specs=(vmem, vmem),
        input_output_aliases={0: 0},
        compiler_params=limit(4),
    )(loaded, partner)
    if direct:

        def across(part, step):
            return lax.ppermute(part, "cols", [(i, i ^ step) for i in range(nb)])

        blocks = [sent] + [None] * 7
        for step in (6, 4, 1, 3, 2):
            blocks[step] = across(sent, step)
        blocks[7] = across(blocks[6], 1)
        blocks[5] = across(blocks[4], 1)
        sides = [blocks[1], blocks[3], blocks[7]]
    else:
        blocks = sides = [lax.all_gather(sent, "cols")]
    kept = pl.pallas_call(
        functools.partial(local, nb, len(sides)),
        out_shape=(shape(128, D), shape(128, D), shape(4, 2 * TW, 2 * NS, dtype=bf16), shape(2, 128, D)),
        in_specs=[vmem] * (9 + len(sides)),
        out_specs=(vmem,) * 4,
        scratch_shapes=[pltpu.VMEM((8, 48, D), f32)],
        compiler_params=limit(16 if direct else 40),
        cost_estimate=pl.CostEstimate(flops=1_000_000_000, bytes_accessed=4_000_000, transcendentals=1_000_000),
    )(sent, far, *sides, w_in, conv_w, conv_b, w_proj, dt_bias, a_rate, d_skip)
    operands = [*blocks, *kept, w_in, conv_w, conv_b, w_proj, dt_bias, a_rate, norm_gain, w_out]
    return pl.pallas_call(
        functools.partial(final, nb, not direct),
        out_shape=shape(TH, TW, D, dtype=bf16),
        in_specs=[vmem] * len(operands),
        out_specs=vmem,
        scratch_shapes=[
            pltpu.VMEM((5, nb * TW + 16, D), f32),
            pltpu.VMEM((nb, 128, D), bf16),
            pltpu.VMEM((nb // 8, 128, 128), f32),
            pltpu.VMEM((nb // 8, 128, 128), f32),
            pltpu.VMEM((nb // 8, 128, 128), f32),
            pltpu.VMEM((4, nb * TW, 128), bf16),
            pltpu.VMEM((4, nb * TW, D), bf16),
        ],
        compiler_params=limit(16 if direct else 48),
        cost_estimate=pl.CostEstimate(flops=1_000_000_000, bytes_accessed=4_000_000, transcendentals=1_000_000),
    )(*operands)


def solution(mesh):
    in_specs = (P(("groups", "rows"), "cols", None), P(), P(), P(), P(), P(), P(), P(), P(), P())
    out_specs = P(("groups", "rows"), "cols", None)
    return jax.shard_map(shards, mesh=mesh, in_specs=in_specs, out_specs=out_specs, check_vma=False)
```

```python
import functools

import jax
import jax.numpy as jnp
from jax import lax
from jax.experimental import pallas as pl
from jax.experimental.pallas import tpu as pltpu
from jax.sharding import PartitionSpec as P

norm_eps = 1e-05
f32, bf16 = jnp.float32, jnp.bfloat16
TH, TW, D, NH, NS = 4, 32, 256, 16, 64
START_ORDER = (6, 4, 3, 1, 2, 7, 5)
FORWARDED = {7: 6, 5: 4}
HALO = 176


def dot(a, b):
    return jnp.dot(a, b, preferred_element_type=f32)


def dot_t(a, b):
    return lax.dot_general(a, b, (((1,), (1,)), ((), ())), preferred_element_type=f32)


def split(a):
    high = a.astype(bf16)
    return high, (a - high.astype(f32)).astype(bf16)


def dot_wide(a, mask):
    high, low = split(a)
    return dot(high, mask) + dot(low, mask)


def wide_dot(mask, b):
    high, low = split(b)
    return dot(mask, high) + dot(mask, low)


def softplus(x):
    return jnp.maximum(x, 0.0) + jnp.log1p(jnp.exp(-jnp.abs(x)))


def silu(x):
    return x * jax.nn.sigmoid(x)


def iotas(rows, lanes):
    return (
        lax.broadcasted_iota(jnp.int32, (rows, lanes), 0),
        lax.broadcasted_iota(jnp.int32, (rows, lanes), 1),
    )


def ones_where(mask):
    return jnp.where(mask, 1.0, 0.0).astype(bf16)


def at(g, j):
    start = g * (8 * TW) + TW * j
    return pl.ds(start if isinstance(start, int) else pl.multiple_of(start, TW), TW)


def each(count, body):
    if count == 1:
        body(0)
    else:
        lax.fori_loop(0, count, lambda i, carry: (body(i), carry)[1], 0)


def load(feats, w_in, conv_w, conv_b, w_proj, dt_bias, a_rate, d_skip, gain, w_out, *refs):
    lower = lax.axis_index("rows") == 1
    sent, outs, sems = refs[0], refs[1:-1], refs[-1]
    copies = [
        pltpu.make_async_copy(
            feats.at[jnp.where(lower, i, 3 - i)], sent.at[pl.ds(TW * (i + 1), TW), :], sems.at[i]
        )
        for i in range(4)
    ]
    weights = (w_in, conv_w, conv_b, w_proj, dt_bias, a_rate, d_skip, gain, w_out)
    copies += [
        pltpu.make_async_copy(source, target, sems.at[4 + i])
        for i, (source, target) in enumerate(zip(weights, outs))
    ]
    for copy in copies:
        copy.start()
    for copy in copies:
        copy.wait()


def pack(loaded, partner, sent, short, far):
    lower = lax.axis_index("rows") == 1
    own = [loaded[TW * (i + 1) : TW * (i + 2), :] for i in range(4)]
    rows = [partner[jnp.where(lower, i, 3 - i)] for i in range(4)] + own
    for i in range(3, 8):
        sent[TW * (i - 3) : TW * (i - 2), :] = rows[i]
        short[TW * (i - 3) : TW * (i - 2), :] = rows[i]
    for i in range(3):
        far[i * TW : (i + 1) * TW, :] = rows[i]
    wide = [part.astype(f32) for part in rows]
    edges = [part[:1] for part in wide] + [part[TW - 1 :] for part in wide]
    sent[160:HALO, :] = jnp.concatenate(edges, axis=0).astype(bf16)


def direction_taps(conv_w, lower):
    return [
        [
            jnp.where(lower, conv_w[3 * a + b : 3 * a + b + 1, :], conv_w[3 * (2 - a) + b : 3 * (2 - a) + b + 1, :])
            for b in range(3)
        ]
        for a in range(3)
    ]


def filtered(ref, count, q, base, taps, bias):
    total = jnp.broadcast_to(bias, (TW, D))
    for a in range(3):
        if 0 <= q + a - 1 < count:
            if not isinstance(base, int):
                cells = ref[q + a - 1, pl.ds(pl.multiple_of(base - 8, 8), TW + 16), :]
            for b in range(3):
                if isinstance(base, int):
                    value = ref[q + a - 1, base + b - 1 : base + b - 1 + TW, :]
                else:
                    value = cells[7 + b : 7 + b + TW]
                total = total + taps[a][b] * value
    return silu(total).astype(bf16)


def filter_row(ref, count, q, columns, shifted, taps, bias):
    def total(b, start, size):
        rows = [a for a in range(3) if 0 <= q + a - 1 < count]
        parts = [taps[a][b] * ref[q + a - 1, start : start + size, :] for a in rows]
        return functools.reduce(jnp.add, parts)

    for start in range(0, columns + 8, TW):
        size = min(TW, columns + 8 - start)
        shifted[0, start : start + size, :] = total(0, start, size)
        shifted[1, start + 8 : start + 8 + size, :] = total(2, start + 8, size)
    out = []
    for start in range(8, columns + 8, TW):
        moved = shifted[0, start - 1 : start - 1 + TW, :] + shifted[1, start + 1 : start + 1 + TW, :]
        out.append(silu(moved + (total(1, start, TW) + bias)).astype(bf16))
    return out


def local(nb, count, sent, far, *refs):
    sides, refs = refs[:count], refs[count:]
    w_in, conv_w, conv_b, w_proj, dt_bias, a_rate, d_skip = refs[:7]
    base_out, gate_out, reads_out, edge_out, strip, shifted = refs[7:]
    row, col = lax.axis_index("rows"), lax.axis_index("cols")
    lower = row == 1
    w_x = w_in[:, :D]

    def pre_conv(tokens):
        return dot(tokens, w_x).astype(bf16).astype(f32)

    if count == 1:
        left = sides[0][jnp.maximum(col - 1, 0), 160:HALO, :]
        right = sides[0][jnp.minimum(col + 1, nb - 1), 160:HALO, :]
    else:
        near, further, furthest = (side[160:HALO, :] for side in sides)
        odd = lax.rem(col, 2) == 1
        left = jnp.where(odd, near, jnp.where(col == 4, furthest, further))
        right = jnp.where(odd, jnp.where(col == 3, furthest, further), near)
    left = pre_conv(left) * jnp.where(col > 0, 1.0, 0.0)
    right = pre_conv(right) * jnp.where(col < nb - 1, 1.0, 0.0)
    far_pre, own_pre = pre_conv(far[...]), pre_conv(sent[0:160, :])
    strip[:, 0:8, :] = jnp.zeros((8, 8, D), f32)
    strip[:, 40:48, :] = jnp.zeros((8, 8, D), f32)
    for i in range(8):
        strip[i, 8:40, :] = far_pre[i * TW : (i + 1) * TW] if i < 3 else own_pre[(i - 3) * TW : (i - 2) * TW]
        strip[i, 7:8, :] = left[8 + i : 9 + i]
        strip[i, 40:41, :] = right[i : i + 1]
    taps, bias = direction_taps(conv_w, lower), conv_b[...]
    strip_mixed = [filter_row(strip, 8, q, TW, shifted.at[q % 2], taps, bias)[0] for q in range(8)]
    own = jnp.concatenate(strip_mixed[4:], axis=0)
    column_tokens = jnp.concatenate(strip_mixed, axis=0)
    gate_out[...] = silu(dot(sent[TW:160, :], w_in[:, D:]))

    head_lane = ones_where(iotas(NH, 128)[1] % NH == iotas(NH, 128)[0])
    expand = ones_where(iotas(NH, D)[1] // NH == iotas(NH, D)[0])
    tok_r, tok_c = iotas(128, 128)
    same_row = tok_r // TW == tok_c // TW
    upto = ones_where(same_row & (tok_c <= tok_r))
    onward = ones_where(same_row & (tok_c >= tok_r))

    projected = [dot_t(own, w_proj[k]) for k in range(2)]
    steps = [softplus(projected[k][:, :NH] + dt_bias[k : k + 1, :]) for k in range(2)]
    logs = [-steps[k] * a_rate[k : k + 1, :] for k in range(2)]
    write = [projected[k][:, NH : NH + NS].astype(bf16) for k in range(2)]
    read = [projected[k][:, NH + NS :].astype(bf16) for k in range(2)]
    reach = [dot(read[k], w_proj[k, NH : NH + NS, :]).astype(bf16) for k in range(2)]
    from_edge = [
        dot_wide(jnp.exp(wide_dot(mask, logs[k])), expand) for k, mask in enumerate((upto, onward))
    ]
    edge_out[0], edge_out[1] = from_edge
    pair_r, pair_c = iotas(NH, NH * TW)
    spread = ones_where(pair_c // TW == pair_r)
    inner_r, inner_c = iotas(128, NH * TW)
    inner_u, inner_s = inner_r % TW, inner_c % TW
    stacked = [part for k in range(2) for part in split(logs[k])] + [part for k in range(2) for part in split(steps[k])]
    wide = dot(jnp.concatenate(stacked, axis=0), spread)
    wide = [wide[i * 128 : (i + 1) * 128] for i in range(8)]
    parts = [
        jnp.where(inner_u > inner_s if i < 2 else inner_u < inner_s, wide[i], 0.0).astype(bf16) for i in range(4)
    ]
    step_parts = [jnp.where(inner_u == inner_s, wide[4 + 2 * k] + wide[5 + 2 * k], 0.0) for k in range(2)]
    time_r, time_c = iotas(TW, TW)
    first, second = ones_where(time_c <= time_r), ones_where(time_c >= time_r)
    walk = jnp.concatenate([first, first, second, second], axis=1)
    local_t, local_s = iotas(TW, NH * TW)
    local_s = local_s % TW
    feature = lax.broadcasted_iota(jnp.int32, (TW, D), 1) // NH
    head_mask = [ones_where(feature == h) for h in range(NH)]
    across = []
    for q in range(4):
        rows = slice(q * TW, (q + 1) * TW)
        gaps = dot(walk, jnp.concatenate([part[rows] for part in parts], axis=0))
        weights = jnp.zeros((TW, NH * TW), f32)
        for k, keep in enumerate((local_s <= local_t, local_s >= local_t)):
            scores = dot_t(read[k][rows], jnp.concatenate([write[k][rows]] * NH, axis=0))
            step_row = jnp.sum(step_parts[k][rows], axis=0, keepdims=True)
            weights = weights + jnp.where(keep, scores * step_row, 0.0)
        weights = (weights * jnp.exp(gaps)).astype(bf16)
        values = own[rows]
        spread_values = jnp.concatenate(
            [values * head_mask[h] for h in range(NH)], axis=0
        )
        result = dot(weights, spread_values)
        reads_out[q] = jnp.concatenate([reach[0][rows], reach[1][rows]], axis=0)
        across.append(result)
    across = jnp.concatenate(across, axis=0)

    k_in = jnp.where(lower, 2, 3)
    k_out = jnp.where(lower, 3, 2)

    def pick_row(ref, k):
        return jnp.where(k == 2, ref[2:3, :], ref[3:4, :])

    project_in = dot_t(column_tokens, w_proj[k_in])
    project_out = dot_t(own, w_proj[k_out])
    steps_in = softplus(project_in[:, :NH] + pick_row(dt_bias, k_in))
    steps_out = softplus(project_out[:, :NH] + pick_row(dt_bias, k_out))
    logs_in = -steps_in * pick_row(a_rate, k_in)
    logs_out = -steps_out * pick_row(a_rate, k_out)
    write_in = project_in[:, NH : NH + NS].astype(bf16)
    write_out = project_out[:, NH : NH + NS].astype(bf16)
    read_in = project_in[128:, NH + NS :].astype(bf16)
    read_out = project_out[:, NH + NS :].astype(bf16)
    t_r, s_c = iotas(128, 256)
    same_col = (t_r % TW) == (s_c % TW)
    meet_in = ones_where(same_col)
    walk_in = ones_where(same_col & (s_c // TW <= t_r // TW + 4))
    meet_out = ones_where(tok_r % TW == tok_c % TW)
    walk_out = ones_where((tok_r % TW == tok_c % TW) & (tok_c >= tok_r))
    source_r, source_c = iotas(256, 128)
    source_u, source_s = source_r // TW, source_c // NH
    select = ones_where(source_u == source_s)
    scores_in = dot_wide(jnp.where(same_col, dot_t(read_in, write_in), 0.0), select)
    same_out = tok_r % TW == tok_c % TW
    scores_out = dot_wide(jnp.where(same_out, dot_t(read_out, write_out), 0.0), select[128:])
    out_u = tok_r // TW + 4
    out_s = tok_c // NH
    gap = jnp.zeros((128, 128), f32)
    for part in split(logs_in):
        gap = gap + dot(walk_in, jnp.where(source_u > source_s, dot(part, head_lane), 0.0).astype(bf16))
    for part in split(logs_out):
        gap = gap + dot(walk_out, jnp.where(out_u < out_s, dot(part, head_lane), 0.0).astype(bf16))
    lane_in = jnp.zeros((128, 128), f32)
    for part in split(steps_in):
        lane_in = lane_in + dot(meet_in, jnp.where(source_u == source_s, dot(part, head_lane), 0.0).astype(bf16))
    lane_out = jnp.zeros((128, 128), f32)
    for part in split(steps_out):
        lane_out = lane_out + dot(meet_out, jnp.where(out_u == out_s, dot(part, head_lane), 0.0).astype(bf16))
    weights = jnp.where(out_s <= out_u, scores_in * lane_in, 0.0) + jnp.where(out_s >= out_u, scores_out * lane_out, 0.0)
    weights = (weights * jnp.exp(gap)).astype(bf16)
    skips = dot_wide(d_skip[...], expand)
    own_wide = own.astype(f32)
    pick_r, pick_c = iotas(128, D)
    vertical = (skips[2:3] + skips[3:4]) * own_wide
    for s in range(8):
        factor = dot(weights, ones_where(pick_r == s * NH + pick_c // NH))
        values = strip_mixed[s].astype(f32)
        vertical = vertical + factor * jnp.concatenate([values] * 4, axis=0)
    base_out[...] = across + (skips[0:1] + skips[1:2]) * own_wide + vertical.astype(bf16).astype(f32)


def final(nb, gathered, *refs):
    count = 1 if gathered else nb
    blocks, refs = refs[:count], refs[count:]
    base_in, gate_in, reads_in, edge_in = refs[:4]
    w_in, conv_w, conv_b, w_proj, dt_bias, a_rate, gain, w_out, out = refs[4:13]
    pre, mixed, la_all, dt_all, totals, attended, scaled = refs[13:]
    row, col = lax.axis_index("rows"), lax.axis_index("cols")
    lower = row == 1
    ng = nb // 8
    w_x = w_in[:, :D]

    def pre_conv(tokens):
        return dot(tokens, w_x).astype(bf16).astype(f32)

    pre[:, 0:8, :] = jnp.zeros((5, 8, D), f32)
    pre[:, 8 + nb * TW :, :] = jnp.zeros((5, 8, D), f32)

    def place_block(tokens, position):
        rows = pre_conv(tokens)
        base = pl.multiple_of(position * TW + 8, 8)
        for q in range(5):
            pre[q, pl.ds(base, TW), :] = rows[q * TW : (q + 1) * TW]

    if gathered:
        each(nb, lambda j: place_block(blocks[0][j, 0:160, :], j))
    else:
        for step in range(nb):
            place_block(blocks[step][0:160, :], col ^ step)
    taps, bias = direction_taps(conv_w, lower), conv_b[...]

    head_lane = ones_where(iotas(NH, 128)[1] % NH == iotas(NH, 128)[0])
    tok_r, tok_c = iotas(128, 128)
    same_row = tok_r // TW == tok_c // TW
    after = ones_where(same_row & (tok_c > tok_r))
    before = ones_where(same_row & (tok_c < tok_r))
    row_ones = ones_where(same_row)
    lane = lax.broadcasted_iota(jnp.int32, (1, 128), 1)
    bias_2 = dot_wide(dt_bias[0:2, :], head_lane)
    rate_2 = dot_wide(a_rate[0:2, :], head_lane)

    def first_pass(g):
        group = lane // NH + g * 8
        is_left = group < col
        w_step = jnp.concatenate(
            [jnp.where(g * 8 + j < col, w_proj[0, 0:NH, :], w_proj[1, 0:NH, :]) for j in range(8)], axis=0
        )
        raw = jnp.zeros((128, 128), f32)
        for j in range(8):
            base = g * (8 * TW) + (8 + TW * j)
            for q in range(1, 5):
                mixed[g * 8 + j, (q - 1) * TW : q * TW, :] = filtered(pre, 5, q, base, taps, bias)
            raw = jnp.where(lane // NH == j, dot_t(mixed[g * 8 + j], w_step), raw)
            block = g * 8 + j
            side = lax.broadcasted_iota(jnp.int32, (1, 2 * TW), 1) < TW
            keep = jnp.where(side, jnp.where(block < col, 1.0, 0.0), jnp.where(block > col, 1.0, 0.0))
            for q in range(4):
                tokens = mixed[g * 8 + j, q * TW : (q + 1) * TW, :]
                attended[q, at(g, j), :] = (dot_t(tokens, reads_in[q]) * keep).astype(bf16)
        steps = softplus(raw + jnp.where(is_left, bias_2[0:1], bias_2[1:2]))
        steps = jnp.where(group == col, 0.0, steps)
        logs = -steps * jnp.where(is_left, rate_2[0:1], rate_2[1:2])
        dt_all[g] = steps
        la_all[g] = logs
        totals[g] = wide_dot(row_ones, logs)

    each(ng, first_pass)

    both_ways = jnp.concatenate([after, before], axis=1)

    def second_pass(g):
        group = lane // NH + g * 8
        logs = la_all[g]
        stacked = jnp.concatenate([jnp.where(group < col, logs, 0.0), jnp.where(group > col, logs, 0.0)], axis=0)
        reach = wide_dot(both_ways, stacked)

        def add_group(other, total):
            source, target = other * 8 + tok_r // NH, g * 8 + tok_c // NH
            nearer = ((source > target) & (source < col)) | ((source < target) & (source > col))
            nearer = nearer & (tok_r % NH == tok_c % NH)
            return total + dot_wide(totals[other], ones_where(nearer))

        if ng == 1:
            reach = add_group(0, reach)
        else:
            reach = lax.fori_loop(0, ng, add_group, reach)
        weight = jnp.concatenate(split(jnp.exp(reach) * dt_all[g]), axis=1)
        expand_r, expand_c = iotas(256, D)
        for j in range(8):
            pick = ones_where((expand_r % 128) == j * NH + expand_c // NH)
            factor = dot(weight, pick)
            values = (mixed[g * 8 + j].astype(f32) * factor).astype(bf16)
            for q in range(4):
                scaled[q, at(g, j), :] = values[q * TW : (q + 1) * TW]

    each(ng, second_pass)

    finish(lower, attended, 0, scaled, base_in, gate_in, edge_in, gain, w_out, out)


def finish(lower, attended, axis, scaled, base_in, gate_in, edge_in, gain, w_out, out):
    entered = []
    for q in range(4):
        rows = slice(q * TW, (q + 1) * TW)
        both = lax.dot_general(attended[q], scaled[q], (((axis,), (0,)), ((), ())), preferred_element_type=f32)
        entered.append(both[:TW] * edge_in[0, rows, :] + both[TW:] * edge_in[1, rows, :])
    combined = base_in[...] + jnp.concatenate(entered, axis=0)

    centre = combined - jnp.mean(combined, axis=-1, keepdims=True)
    normed = centre * lax.rsqrt(jnp.mean(centre * centre, axis=-1, keepdims=True) + norm_eps) * gain[...]
    gated = (normed * gate_in[...]).astype(bf16)
    result = dot(gated, w_out[...]).astype(bf16)
    for i in range(4):
        out[jnp.where(lower, i, 3 - i)] = result[i * TW : (i + 1) * TW]


def early(sent, first, second, third, w_in, conv_w, conv_b, pre, mixed, shifted):
    col = lax.axis_index("cols")
    lower = lax.axis_index("rows") == 1
    w_x = w_in[:, :D]
    pre[:, 0:8, :] = jnp.zeros((5, 8, D), f32)
    pre[:, 136:144, :] = jnp.zeros((5, 8, D), f32)
    for step, block in enumerate((sent, first, second, third)):
        place_rows(pre, block, w_x, (col & 3) ^ step)
    taps, bias = direction_taps(conv_w, lower), conv_b[...]
    for q in range(1, 5):
        for j, part in enumerate(filter_row(pre, 5, q, 128, shifted.at[q % 2], taps, bias)):
            mixed[q - 1, TW * j : TW * (j + 1), :] = part


def place_rows(pre, block, w_x, position):
    rows = dot(block[0:160, :], w_x).astype(bf16).astype(f32)
    base = pl.multiple_of(position * TW + 8, 8)
    for q in range(5):
        pre[q, pl.ds(base, TW), :] = rows[q * TW : (q + 1) * TW]


def late(*refs):
    blocks, (half_pre, half_mixed, base_in, gate_in, reads_in, edge_in), refs = refs[:4], refs[4:10], refs[10:]
    w_in, conv_w, conv_b, w_proj, dt_bias, a_rate, gain, w_out, out = refs[:9]
    pre, mixed, attended, scaled, pick, shifted = refs[9:]
    pre[:, 0:8, :] = jnp.zeros((5, 8, D), f32)
    pre[:, 136:144, :] = jnp.zeros((5, 8, D), f32)
    row, col = lax.axis_index("rows"), lax.axis_index("cols")
    lower = row == 1
    on_left = col < 4
    w_x = w_in[:, :D]
    for step, block in enumerate(blocks):
        place_rows(pre, block, w_x, (col & 3) ^ step)
    zero = jnp.zeros((1, D), f32)
    for q in range(5):
        pre[q, 7:8, :] = jnp.where(on_left, half_pre[q, 135:136, :], zero)
        pre[q, 136:137, :] = jnp.where(on_left, zero, half_pre[q, 8:9, :])
    taps, bias = direction_taps(conv_w, lower), conv_b[...]
    for q in range(4):
        for j, part in enumerate(filter_row(pre, 5, q + 1, 128, shifted.at[q % 2], taps, bias)):
            mixed[q, 128 + TW * j : 128 + TW * (j + 1), :] = part
    tile = lax.broadcasted_iota(jnp.int32, (16, D), 0)
    low_place, high_place = jnp.where(on_left, 16, 0), jnp.where(on_left, 15, 16)
    for q in range(4):
        total = bias
        for a in range(3):
            if q + a < 5:
                at_left = (half_pre[q + a, 134:135, :], half_pre[q + a, 135:136, :], pre[q + a, 8:9, :])
                at_right = (pre[q + a, 135:136, :], half_pre[q + a, 8:9, :], half_pre[q + a, 9:10, :])
                for b in range(3):
                    total = total + taps[a][b] * jnp.where(on_left, at_left[b], at_right[b])
        value = silu(total)
        mixed[q, 16:112, :] = half_mixed[q, 16:112, :]
        for start, place in ((0, low_place), (112, high_place)):
            held = half_mixed[q, start : start + 16, :].astype(f32)
            mixed[q, start : start + 16, :] = jnp.where(tile == place, value, held).astype(bf16)

    turn = jnp.where(on_left, 0, 4)
    head_lane = ones_where(iotas(NH, 128)[1] % NH == iotas(NH, 128)[0])
    tok_r, tok_c = iotas(128, 128)
    same_row = tok_r // TW == tok_c // TW
    after = ones_where(same_row & (tok_c > tok_r))
    before = ones_where(same_row & (tok_c < tok_r))
    row_ones = ones_where(same_row)
    lane = lax.broadcasted_iota(jnp.int32, (1, 128), 1)
    group = (lane // NH) ^ turn
    is_left = group < col
    bias_2 = dot_wide(dt_bias[0:2, :], head_lane)
    rate_2 = dot_wide(a_rate[0:2, :], head_lane)
    w_step = jnp.concatenate(
        [jnp.where((j ^ turn) < col, w_proj[0, 0:NH, :], w_proj[1, 0:NH, :]) for j in range(8)], axis=0
    )
    side, block = iotas(2 * TW, 256)
    block = (block // TW) ^ turn
    keep = jnp.where(side < TW, jnp.where(block < col, 1.0, 0.0), jnp.where(block > col, 1.0, 0.0))
    raw = []
    for q in range(4):
        result = dot_t(mixed[q], w_step)
        row_raw = result[0:TW]
        for j in range(1, 8):
            row_raw = jnp.where(lane // NH == j, result[TW * j : TW * (j + 1)], row_raw)
        raw.append(row_raw)
        attended[q] = (dot_t(reads_in[q], mixed[q]) * keep).astype(bf16)
    raw = jnp.concatenate(raw, axis=0)
    steps = softplus(raw + jnp.where(is_left, bias_2[0:1], bias_2[1:2]))
    steps = jnp.where(group == col, 0.0, steps)
    logs = -steps * jnp.where(is_left, rate_2[0:1], rate_2[1:2])
    source, target = (tok_r // NH) ^ turn, (tok_c // NH) ^ turn
    nearer = ((source > target) & (source < col)) | ((source < target) & (source > col))
    reach = dot_wide(wide_dot(row_ones, logs), ones_where(nearer & (tok_r % NH == tok_c % NH)))
    reach = reach + wide_dot(after, jnp.where(is_left, logs, 0.0)) + wide_dot(before, jnp.where(is_left, 0.0, logs))
    weight = split(jnp.exp(reach) * steps)
    pick[0:112, :] = jnp.zeros((112, D), bf16)
    pick[112:128, :] = ones_where(iotas(NH, D)[1] // NH == iotas(NH, D)[0])
    pick[128:240, :] = jnp.zeros((112, D), bf16)
    for j in range(8):
        mask = pick[112 - NH * j : 240 - NH * j, :]
        factor = dot(weight[0], mask) + dot(weight[1], mask)
        for q in range(4):
            cells = slice(TW * j, TW * (j + 1))
            scaled[q, cells, :] = (mixed[q, cells, :].astype(f32) * factor[q * TW : (q + 1) * TW]).astype(bf16)
    finish(lower, attended, 1, scaled, base_in, gate_in, edge_in, gain, w_out, out)


def shards(feats, w_in, conv_w, conv_b, w_proj, dt_bias, a_rate, d_skip, norm_gain, w_out):
    nb = lax.axis_size("cols")
    direct = nb == 8
    vmem, hbm = pl.BlockSpec(memory_space=pltpu.VMEM), pl.BlockSpec(memory_space=pltpu.HBM)

    def shape(*dims, dtype=f32):
        return jax.ShapeDtypeStruct(dims, dtype)

    def limit(mib):
        return pltpu.CompilerParams(vmem_limit_bytes=mib << 20)

    partner = lax.ppermute(feats, "rows", [(0, 1), (1, 0)])
    params = [w_in, conv_w, conv_b[None], jnp.swapaxes(w_proj, 1, 2), dt_bias, a_rate, d_skip, norm_gain[None], w_out]
    loaded, *params = pl.pallas_call(
        load,
        out_shape=(shape(HALO, D, dtype=bf16), *[shape(*part.shape, dtype=part.dtype) for part in params]),
        in_specs=[hbm] * 10,
        out_specs=(vmem,) * 10,
        scratch_shapes=[pltpu.SemaphoreType.DMA((13,))],
        compiler_params=limit(8),
    )(*[pltpu.with_memory_space_constraint(part, pltpu.HBM) for part in (feats, *params)])
    w_in, conv_w, conv_b, w_proj, dt_bias, a_rate, d_skip, norm_gain, w_out = params
    sent, short, far = pl.pallas_call(
        pack,
        out_shape=tuple(shape(count, D, dtype=bf16) for count in (HALO, 160, 96)),
        in_specs=[vmem] * 2,
        out_specs=(vmem,) * 3,
        input_output_aliases={0: 0},
        compiler_params=limit(4),
    )(loaded, partner)
    if direct:

        def across(part, step):
            return lax.ppermute(part, "cols", [(i, i ^ step) for i in range(nb)])

        blocks = [sent] + [None] * 7
        for block in START_ORDER:
            source = FORWARDED.get(block)
            own = short if block in (2, 4) else sent
            blocks[block] = across(own, block) if source is None else across(blocks[source], block ^ source)
        sides = [blocks[1], blocks[3], blocks[7]]
    else:
        blocks = sides = [lax.all_gather(sent, "cols")]
    kept = pl.pallas_call(
        functools.partial(local, nb, len(sides)),
        out_shape=(shape(128, D), shape(128, D), shape(4, 2 * TW, D, dtype=bf16), shape(2, 128, D)),
        in_specs=[vmem] * (9 + len(sides)),
        out_specs=(vmem,) * 4,
        scratch_shapes=[pltpu.VMEM((8, 48, D), f32), pltpu.VMEM((2, 2, 48, D), f32)],
        compiler_params=limit(16 if direct else 40),
        cost_estimate=pl.CostEstimate(flops=1_000_000_000, bytes_accessed=4_000_000, transcendentals=1_000_000),
    )(sent, far, *sides, w_in, conv_w, conv_b, w_proj, dt_bias, a_rate, d_skip)
    tail = [w_in, conv_w, conv_b, w_proj, dt_bias, a_rate, norm_gain, w_out]
    if direct:
        half = pl.pallas_call(
            early,
            out_shape=(shape(5, 144, D), shape(4, 128, D, dtype=bf16)),
            in_specs=[vmem] * 7,
            out_specs=(vmem,) * 2,
            scratch_shapes=[pltpu.VMEM((2, 2, 144, D), f32)],
            compiler_params=limit(8),
            cost_estimate=pl.CostEstimate(flops=200_000_000, bytes_accessed=1_500_000, transcendentals=200_000),
        )(*blocks[:4], w_in, conv_w, conv_b)
        operands = [*blocks[4:], *half, *kept, *tail]
        body = late
        scratch = [
            pltpu.VMEM((5, 144, D), f32),
            pltpu.VMEM((4, 256, D), bf16),
            pltpu.VMEM((4, 2 * TW, 256), bf16),
            pltpu.VMEM((4, 256, D), bf16),
            pltpu.VMEM((240, D), bf16),
            pltpu.VMEM((2, 2, 144, D), f32),
        ]
    else:
        operands = [*blocks, *kept, *tail]
        body = functools.partial(final, nb, True)
        scratch = [
            pltpu.VMEM((5, nb * TW + 16, D), f32),
            pltpu.VMEM((nb, 128, D), bf16),
            pltpu.VMEM((nb // 8, 128, 128), f32),
            pltpu.VMEM((nb // 8, 128, 128), f32),
            pltpu.VMEM((nb // 8, 128, 128), f32),
            pltpu.VMEM((4, nb * TW, 2 * TW), bf16),
            pltpu.VMEM((4, nb * TW, D), bf16),
        ]
    return pl.pallas_call(
        body,
        out_shape=shape(TH, TW, D, dtype=bf16),
        in_specs=[vmem] * len(operands),
        out_specs=vmem,
        scratch_shapes=scratch,
        compiler_params=limit(16 if direct else 48),
        cost_estimate=pl.CostEstimate(flops=1_000_000_000, bytes_accessed=4_000_000, transcendentals=1_000_000),
    )(*operands)


def solution(mesh):
    in_specs = (P(("groups", "rows"), "cols", None), P(), P(), P(), P(), P(), P(), P(), P(), P())
    out_specs = P(("groups", "rows"), "cols", None)
    return jax.shard_map(shards, mesh=mesh, in_specs=in_specs, out_specs=out_specs, check_vma=False)
```

```python
import functools

import jax
import jax.numpy as jnp
from jax import lax
from jax.experimental import pallas as pl
from jax.experimental.pallas import tpu as pltpu
from jax.sharding import PartitionSpec as P

norm_eps = 1e-05
f32, bf16 = jnp.float32, jnp.bfloat16
TH, TW, D, NH, NS = 4, 32, 256, 16, 64
START_ORDER = (6, 4, 3, 1, 2, 7, 5)
FORWARDED = {7: 6, 5: 4}
HALO = 176


def dot(a, b):
    return jnp.dot(a, b, preferred_element_type=f32)


def dot_t(a, b):
    return lax.dot_general(a, b, (((1,), (1,)), ((), ())), preferred_element_type=f32)


def split(a):
    high = a.astype(bf16)
    return high, (a - high.astype(f32)).astype(bf16)


def dot_wide(a, mask):
    high, low = split(a)
    return dot(high, mask) + dot(low, mask)


def wide_dot(mask, b):
    high, low = split(b)
    return dot(mask, high) + dot(mask, low)


def softplus(x):
    return jnp.maximum(x, 0.0) + jnp.log1p(jnp.exp(-jnp.abs(x)))


def silu(x):
    return x * jax.nn.sigmoid(x)


def iotas(rows, lanes):
    return (
        lax.broadcasted_iota(jnp.int32, (rows, lanes), 0),
        lax.broadcasted_iota(jnp.int32, (rows, lanes), 1),
    )


def ones_where(mask):
    return jnp.where(mask, 1.0, 0.0).astype(bf16)


def at(g, j):
    start = g * (8 * TW) + TW * j
    return pl.ds(start if isinstance(start, int) else pl.multiple_of(start, TW), TW)


def each(count, body):
    if count == 1:
        body(0)
    else:
        lax.fori_loop(0, count, lambda i, carry: (body(i), carry)[1], 0)


def load(feats, w_in, conv_w, conv_b, w_proj, dt_bias, a_rate, d_skip, gain, w_out, *refs):
    lower = lax.axis_index("rows") == 1
    sent, outs, sems = refs[0], refs[1:-1], refs[-1]
    copies = [
        pltpu.make_async_copy(
            feats.at[jnp.where(lower, i, 3 - i)], sent.at[pl.ds(TW * (i + 1), TW), :], sems.at[i]
        )
        for i in range(4)
    ]
    weights = (w_in, conv_w, conv_b, w_proj, dt_bias, a_rate, d_skip, gain, w_out)
    copies += [
        pltpu.make_async_copy(source, target, sems.at[4 + i])
        for i, (source, target) in enumerate(zip(weights, outs))
    ]
    for copy in copies:
        copy.start()
    for copy in copies:
        copy.wait()


def pack(loaded, partner, sent, short, far):
    lower = lax.axis_index("rows") == 1
    own = [loaded[TW * (i + 1) : TW * (i + 2), :] for i in range(4)]
    rows = [partner[jnp.where(lower, i, 3 - i)] for i in range(4)] + own
    for i in range(3, 8):
        sent[TW * (i - 3) : TW * (i - 2), :] = rows[i]
        short[TW * (i - 3) : TW * (i - 2), :] = rows[i]
    for i in range(3):
        far[i * TW : (i + 1) * TW, :] = rows[i]
    wide = [part.astype(f32) for part in rows]
    edges = [part[:1] for part in wide] + [part[TW - 1 :] for part in wide]
    sent[160:HALO, :] = jnp.concatenate(edges, axis=0).astype(bf16)


def direction_taps(conv_w, lower):
    return [
        [
            jnp.where(lower, conv_w[3 * a + b : 3 * a + b + 1, :], conv_w[3 * (2 - a) + b : 3 * (2 - a) + b + 1, :])
            for b in range(3)
        ]
        for a in range(3)
    ]


def filtered(ref, count, q, base, taps, bias):
    total = jnp.broadcast_to(bias, (TW, D))
    for a in range(3):
        if 0 <= q + a - 1 < count:
            if not isinstance(base, int):
                cells = ref[q + a - 1, pl.ds(pl.multiple_of(base - 8, 8), TW + 16), :]
            for b in range(3):
                if isinstance(base, int):
                    value = ref[q + a - 1, base + b - 1 : base + b - 1 + TW, :]
                else:
                    value = cells[7 + b : 7 + b + TW]
                total = total + taps[a][b] * value
    return silu(total).astype(bf16)


def filter_row(ref, count, q, columns, shifted, taps, bias):
    def total(b, start, size):
        rows = [a for a in range(3) if 0 <= q + a - 1 < count]
        parts = [taps[a][b] * ref[q + a - 1, start : start + size, :] for a in rows]
        return functools.reduce(jnp.add, parts)

    for start in range(0, columns + 8, TW):
        size = min(TW, columns + 8 - start)
        shifted[0, start : start + size, :] = total(0, start, size)
        shifted[1, start + 8 : start + 8 + size, :] = total(2, start + 8, size)
    out = []
    for start in range(8, columns + 8, TW):
        moved = shifted[0, start - 1 : start - 1 + TW, :] + shifted[1, start + 1 : start + 1 + TW, :]
        out.append(silu(moved + (total(1, start, TW) + bias)).astype(bf16))
    return out


def ahead(sent, far, w_in, w_proj, dt_bias, a_rate, *outs):
    strip_pre, gate_out, triangle, spread_out, heads_out, select_out, same_out, walk_in, walk_out = outs[:9]
    col = lax.axis_index("cols")
    w_x = w_in[:, :D]
    far_pre = dot(far[...], w_x).astype(bf16).astype(f32)
    own_pre = dot(sent[0:160, :], w_x).astype(bf16).astype(f32)
    for i in range(8):
        strip_pre[i] = far_pre[i * TW : (i + 1) * TW] if i < 3 else own_pre[(i - 3) * TW : (i - 2) * TW]
    gate_out[...] = silu(dot(sent[TW:160, :], w_in[:, D:]))
    inner_u, inner_s = iotas(TW, NH * TW)
    inner_s = inner_s % TW
    for i, mask in enumerate((inner_u > inner_s, inner_u < inner_s, inner_u == inner_s)):
        triangle[i] = jnp.where(mask, 1.0, 0.0)
    pair_r, pair_c = iotas(NH, NH * TW)
    spread_out[...] = ones_where(pair_c // TW == pair_r)
    feature = iotas(TW, D)[1] // NH
    for h in range(NH):
        heads_out[h] = ones_where(feature == h)
    source_r, source_c = iotas(256, 128)
    select_out[...] = ones_where(source_r // TW == source_c // NH)
    t_r, s_c = iotas(128, 256)
    same_out[...] = jnp.where((t_r % TW) == (s_c % TW), 1.0, 0.0)
    walk_r, walk_c = iotas(128, 512)
    step, source, time = walk_r // NH, (walk_c % 128) // NH, walk_c // 128 + 4
    same_head = walk_r % NH == walk_c % NH
    walk_in[...] = ones_where(same_head & (source < step) & (step <= time))
    walk_out[...] = ones_where(same_head & (time <= step) & (step < source))
    if len(outs) == 9:
        return
    ordered, nearer_out, keep_out, pick, w_step, lanes = outs[9:]
    turn = jnp.where(col < 4, 0, 4)
    tok_r, tok_c = iotas(128, 128)
    same_row = tok_r // TW == tok_c // TW
    ordered[0] = ones_where(same_row & (tok_c > tok_r))
    ordered[1] = ones_where(same_row & (tok_c < tok_r))
    ordered[2] = ones_where(same_row)
    source, target = (tok_r // NH) ^ turn, (tok_c // NH) ^ turn
    nearer = ((source > target) & (source < col)) | ((source < target) & (source > col))
    nearer_out[...] = ones_where(nearer & (tok_r % NH == tok_c % NH))
    side, block = iotas(2 * TW, 256)
    block = (block // TW) ^ turn
    keep_out[...] = jnp.where(side < TW, jnp.where(block < col, 1.0, 0.0), jnp.where(block > col, 1.0, 0.0))
    pick[0:112, :] = jnp.zeros((112, D), bf16)
    pick[112:128, :] = ones_where(iotas(NH, D)[1] // NH == iotas(NH, D)[0])
    pick[128:240, :] = jnp.zeros((112, D), bf16)
    w_step[...] = jnp.concatenate(
        [jnp.where((j ^ turn) < col, w_proj[0, 0:NH, :], w_proj[1, 0:NH, :]) for j in range(8)], axis=0
    )
    lane = lax.broadcasted_iota(jnp.int32, (1, 128), 1)
    group = (lane // NH) ^ turn
    head_lane = ones_where(iotas(NH, 128)[1] % NH == iotas(NH, 128)[0])
    bias, rate = dot_wide(dt_bias[0:2, :], head_lane), dot_wide(a_rate[0:2, :], head_lane)
    lanes[0:1, :] = jnp.where(group < col, bias[0:1], bias[1:2])
    lanes[1:2, :] = jnp.where(group < col, rate[0:1], rate[1:2])
    lanes[2:3, :] = jnp.where(group < col, 1.0, 0.0)
    lanes[3:4, :] = jnp.where(group > col, 1.0, 0.0)


def local(nb, count, *refs):
    sides, refs = refs[:count], refs[count:]
    w_in, conv_w, conv_b, w_proj, dt_bias, a_rate, d_skip = refs[:7]
    strip_pre, triangle, spread, heads, select, same_col, walk_in, walk_out = refs[7:15]
    base_out, reads_out, edge_out, strip, shifted = refs[15:]
    row, col = lax.axis_index("rows"), lax.axis_index("cols")
    lower = row == 1
    w_x = w_in[:, :D]

    def pre_conv(tokens):
        return dot(tokens, w_x).astype(bf16).astype(f32)

    if count == 1:
        left = sides[0][jnp.maximum(col - 1, 0), 160:HALO, :]
        right = sides[0][jnp.minimum(col + 1, nb - 1), 160:HALO, :]
    else:
        near, further, furthest = (side[160:HALO, :] for side in sides)
        odd = lax.rem(col, 2) == 1
        left = jnp.where(odd, near, jnp.where(col == 4, furthest, further))
        right = jnp.where(odd, jnp.where(col == 3, furthest, further), near)
    left = pre_conv(left) * jnp.where(col > 0, 1.0, 0.0)
    right = pre_conv(right) * jnp.where(col < nb - 1, 1.0, 0.0)
    strip[:, 0:8, :] = jnp.zeros((8, 8, D), f32)
    strip[:, 40:48, :] = jnp.zeros((8, 8, D), f32)
    for i in range(8):
        strip[i, 8:40, :] = strip_pre[i]
        strip[i, 7:8, :] = left[8 + i : 9 + i]
        strip[i, 40:41, :] = right[i : i + 1]
    taps, bias = direction_taps(conv_w, lower), conv_b[...]
    strip_mixed = [filter_row(strip, 8, q, TW, shifted.at[q % 2], taps, bias)[0] for q in range(8)]
    own = jnp.concatenate(strip_mixed[4:], axis=0)
    column_tokens = jnp.concatenate(strip_mixed, axis=0)

    head_lane = ones_where(iotas(NH, 128)[1] % NH == iotas(NH, 128)[0])
    expand = ones_where(iotas(NH, D)[1] // NH == iotas(NH, D)[0])
    tok_r, tok_c = iotas(128, 128)
    same_row = tok_r // TW == tok_c // TW
    upto = ones_where(same_row & (tok_c <= tok_r))
    onward = ones_where(same_row & (tok_c >= tok_r))

    projected = [dot_t(own, w_proj[k]) for k in range(2)]
    steps = [softplus(projected[k][:, :NH] + dt_bias[k : k + 1, :]) for k in range(2)]
    logs = [-steps[k] * a_rate[k : k + 1, :] for k in range(2)]
    write = [projected[k][:, NH : NH + NS].astype(bf16) for k in range(2)]
    read = [projected[k][:, NH + NS :].astype(bf16) for k in range(2)]
    reach = [dot(read[k], w_proj[k, NH : NH + NS, :]).astype(bf16) for k in range(2)]
    from_edge = [
        dot_wide(jnp.exp(wide_dot(mask, logs[k])), expand) for k, mask in enumerate((upto, onward))
    ]
    edge_out[0], edge_out[1] = from_edge
    stacked = [part for k in range(2) for part in split(logs[k])] + [part for k in range(2) for part in split(steps[k])]
    wide = dot(jnp.concatenate(stacked, axis=0), spread[...])
    wide = [wide[i * 128 : (i + 1) * 128] for i in range(8)]
    later, sooner, equal = triangle[0], triangle[1], triangle[2]
    time_r, time_c = iotas(TW, TW)
    first, second = ones_where(time_c <= time_r), ones_where(time_c >= time_r)
    walk = jnp.concatenate([first, first, second, second], axis=1)
    allowed = (later + equal, sooner + equal)
    across = []
    for q in range(4):
        rows = slice(q * TW, (q + 1) * TW)
        parts = [(wide[i][rows] * (later if i < 2 else sooner)).astype(bf16) for i in range(4)]
        gaps = dot(walk, jnp.concatenate(parts, axis=0))
        weights = jnp.zeros((TW, NH * TW), f32)
        for k, keep in enumerate(allowed):
            scores = dot_t(read[k][rows], jnp.concatenate([write[k][rows]] * NH, axis=0))
            step_row = jnp.sum((wide[4 + 2 * k][rows] + wide[5 + 2 * k][rows]) * equal, axis=0, keepdims=True)
            weights = weights + scores * step_row * keep
        weights = (weights * jnp.exp(gaps)).astype(bf16)
        values = own[rows]
        spread_values = jnp.concatenate(
            [values * heads[h] for h in range(NH)], axis=0
        )
        result = dot(weights, spread_values)
        reads_out[q] = jnp.concatenate([reach[0][rows], reach[1][rows]], axis=0)
        across.append(result)
    across = jnp.concatenate(across, axis=0)

    k_in = jnp.where(lower, 2, 3)
    k_out = jnp.where(lower, 3, 2)

    def pick_row(ref, k):
        return jnp.where(k == 2, ref[2:3, :], ref[3:4, :])

    lane = lax.broadcasted_iota(jnp.int32, (1, 128), 1) // NH
    head_rows = [dot_wide(pick_row(ref, k), head_lane) for ref in (dt_bias, a_rate) for k in (k_in, k_out)]

    def dense_steps(tokens, k, first, bias):
        result = dot_t(tokens, jnp.concatenate([w_proj[k, 0:NH, :]] * 8, axis=0))
        raw = result[0:TW]
        for s in range(first + 1, 8):
            raw = jnp.where(lane == s, result[(s - first) * TW : (s - first + 1) * TW], raw)
        return softplus(raw + bias)

    steps_in = dense_steps(column_tokens, k_in, 0, head_rows[0])
    steps_out = dense_steps(own, k_out, 4, head_rows[1])
    gap = dot(jnp.concatenate(split(-steps_in * head_rows[2]), axis=0), walk_in[...])
    gap_out = dot(jnp.concatenate(split(-steps_out * head_rows[3]), axis=0), walk_out[...])
    gap = (gap[:TW] + gap[TW:]) + (gap_out[:TW] + gap_out[TW:])
    decay = jnp.exp(gap)
    write_in = dot_t(column_tokens, w_proj[k_in, NH : NH + NS, :]).astype(bf16)
    write_out = dot_t(own, w_proj[k_out, NH : NH + NS, :]).astype(bf16)
    read_in = dot_t(own, w_proj[k_in, NH + NS :, :]).astype(bf16)
    read_out = dot_t(own, w_proj[k_out, NH + NS :, :]).astype(bf16)
    scores_in = dot_wide(dot_t(read_in, write_in) * same_col[...], select[...])
    scores_out = dot_wide(dot_t(read_out, write_out) * same_col[:, :128], select[128:, :])
    weights = []
    for t in range(4):
        rows = slice(t * TW, (t + 1) * TW)
        sum_in = scores_in[rows] * (steps_in * jnp.where(lane <= t + 4, 1.0, 0.0))
        sum_out = scores_out[rows] * (steps_out * jnp.where(lane >= t + 4, 1.0, 0.0))
        weights.append((sum_in + sum_out) * decay[:, t * 128 : (t + 1) * 128])
    weights = jnp.concatenate(weights, axis=0).astype(bf16)
    skips = dot_wide(d_skip[...], expand)
    own_wide = own.astype(f32)
    pick_r, pick_c = iotas(128, D)
    pick_c = pick_c // NH
    vertical = (skips[2:3] + skips[3:4]) * own_wide
    for s in range(8):
        factor = dot(weights, ones_where(pick_r == s * NH + pick_c))
        values = strip_mixed[s].astype(f32)
        vertical = vertical + factor * jnp.concatenate([values] * 4, axis=0)
    base_out[...] = across + (skips[0:1] + skips[1:2]) * own_wide + vertical.astype(bf16).astype(f32)


def final(nb, gathered, *refs):
    count = 1 if gathered else nb
    blocks, refs = refs[:count], refs[count:]
    base_in, reads_in, edge_in, gate_in = refs[:4]
    w_in, conv_w, conv_b, w_proj, dt_bias, a_rate, gain, w_out, out = refs[4:13]
    pre, mixed, la_all, dt_all, totals, attended, scaled = refs[13:]
    row, col = lax.axis_index("rows"), lax.axis_index("cols")
    lower = row == 1
    ng = nb // 8
    w_x = w_in[:, :D]

    def pre_conv(tokens):
        return dot(tokens, w_x).astype(bf16).astype(f32)

    pre[:, 0:8, :] = jnp.zeros((5, 8, D), f32)
    pre[:, 8 + nb * TW :, :] = jnp.zeros((5, 8, D), f32)

    def place_block(tokens, position):
        rows = pre_conv(tokens)
        base = pl.multiple_of(position * TW + 8, 8)
        for q in range(5):
            pre[q, pl.ds(base, TW), :] = rows[q * TW : (q + 1) * TW]

    if gathered:
        each(nb, lambda j: place_block(blocks[0][j, 0:160, :], j))
    else:
        for step in range(nb):
            place_block(blocks[step][0:160, :], col ^ step)
    taps, bias = direction_taps(conv_w, lower), conv_b[...]

    head_lane = ones_where(iotas(NH, 128)[1] % NH == iotas(NH, 128)[0])
    tok_r, tok_c = iotas(128, 128)
    same_row = tok_r // TW == tok_c // TW
    after = ones_where(same_row & (tok_c > tok_r))
    before = ones_where(same_row & (tok_c < tok_r))
    row_ones = ones_where(same_row)
    lane = lax.broadcasted_iota(jnp.int32, (1, 128), 1)
    bias_2 = dot_wide(dt_bias[0:2, :], head_lane)
    rate_2 = dot_wide(a_rate[0:2, :], head_lane)

    def first_pass(g):
        group = lane // NH + g * 8
        is_left = group < col
        w_step = jnp.concatenate(
            [jnp.where(g * 8 + j < col, w_proj[0, 0:NH, :], w_proj[1, 0:NH, :]) for j in range(8)], axis=0
        )
        raw = jnp.zeros((128, 128), f32)
        for j in range(8):
            base = g * (8 * TW) + (8 + TW * j)
            for q in range(1, 5):
                mixed[g * 8 + j, (q - 1) * TW : q * TW, :] = filtered(pre, 5, q, base, taps, bias)
            raw = jnp.where(lane // NH == j, dot_t(mixed[g * 8 + j], w_step), raw)
            block = g * 8 + j
            side = lax.broadcasted_iota(jnp.int32, (1, 2 * TW), 1) < TW
            keep = jnp.where(side, jnp.where(block < col, 1.0, 0.0), jnp.where(block > col, 1.0, 0.0))
            for q in range(4):
                tokens = mixed[g * 8 + j, q * TW : (q + 1) * TW, :]
                attended[q, at(g, j), :] = (dot_t(tokens, reads_in[q]) * keep).astype(bf16)
        steps = softplus(raw + jnp.where(is_left, bias_2[0:1], bias_2[1:2]))
        steps = jnp.where(group == col, 0.0, steps)
        logs = -steps * jnp.where(is_left, rate_2[0:1], rate_2[1:2])
        dt_all[g] = steps
        la_all[g] = logs
        totals[g] = wide_dot(row_ones, logs)

    each(ng, first_pass)

    both_ways = jnp.concatenate([after, before], axis=1)

    def second_pass(g):
        group = lane // NH + g * 8
        logs = la_all[g]
        stacked = jnp.concatenate([jnp.where(group < col, logs, 0.0), jnp.where(group > col, logs, 0.0)], axis=0)
        reach = wide_dot(both_ways, stacked)

        def add_group(other, total):
            source, target = other * 8 + tok_r // NH, g * 8 + tok_c // NH
            nearer = ((source > target) & (source < col)) | ((source < target) & (source > col))
            nearer = nearer & (tok_r % NH == tok_c % NH)
            return total + dot_wide(totals[other], ones_where(nearer))

        if ng == 1:
            reach = add_group(0, reach)
        else:
            reach = lax.fori_loop(0, ng, add_group, reach)
        weight = jnp.concatenate(split(jnp.exp(reach) * dt_all[g]), axis=1)
        expand_r, expand_c = iotas(256, D)
        for j in range(8):
            pick = ones_where((expand_r % 128) == j * NH + expand_c // NH)
            factor = dot(weight, pick)
            values = (mixed[g * 8 + j].astype(f32) * factor).astype(bf16)
            for q in range(4):
                scaled[q, at(g, j), :] = values[q * TW : (q + 1) * TW]

    each(ng, second_pass)

    finish(lower, attended, 0, scaled, base_in, gate_in, edge_in, gain, w_out, out)


def finish(lower, attended, axis, scaled, base_in, gate_in, edge_in, gain, w_out, out):
    entered = []
    for q in range(4):
        rows = slice(q * TW, (q + 1) * TW)
        both = lax.dot_general(attended[q], scaled[q], (((axis,), (0,)), ((), ())), preferred_element_type=f32)
        entered.append(both[:TW] * edge_in[0, rows, :] + both[TW:] * edge_in[1, rows, :])
    combined = base_in[...] + jnp.concatenate(entered, axis=0)

    centre = combined - jnp.mean(combined, axis=-1, keepdims=True)
    normed = centre * lax.rsqrt(jnp.mean(centre * centre, axis=-1, keepdims=True) + norm_eps) * gain[...]
    gated = (normed * gate_in[...]).astype(bf16)
    result = dot(gated, w_out[...]).astype(bf16)
    for i in range(4):
        out[jnp.where(lower, i, 3 - i)] = result[i * TW : (i + 1) * TW]


def early(sent, first, second, third, w_in, conv_w, conv_b, pre, mixed, shifted):
    col = lax.axis_index("cols")
    lower = lax.axis_index("rows") == 1
    w_x = w_in[:, :D]
    pre[:, 0:8, :] = jnp.zeros((5, 8, D), f32)
    pre[:, 136:144, :] = jnp.zeros((5, 8, D), f32)
    for step, block in enumerate((sent, first, second, third)):
        place_rows(pre, block, w_x, (col & 3) ^ step)
    taps, bias = direction_taps(conv_w, lower), conv_b[...]
    for q in range(1, 5):
        for j, part in enumerate(filter_row(pre, 5, q, 128, shifted.at[q % 2], taps, bias)):
            mixed[q - 1, TW * j : TW * (j + 1), :] = part


def place_rows(pre, block, w_x, position):
    rows = dot(block[0:160, :], w_x).astype(bf16).astype(f32)
    base = pl.multiple_of(position * TW + 8, 8)
    for q in range(5):
        pre[q, pl.ds(base, TW), :] = rows[q * TW : (q + 1) * TW]


def late(*refs):
    blocks, (half_pre, half_mixed, base_in, reads_in, edge_in, gate_in), refs = refs[:4], refs[4:10], refs[10:]
    ordered, nearer, keep, pick, w_step, lanes = refs[:6]
    refs = refs[6:]
    w_in, conv_w, conv_b, _, _, _, gain, w_out, out = refs[:9]
    pre, mixed, attended, scaled, shifted = refs[9:]
    pre[:, 0:8, :] = jnp.zeros((5, 8, D), f32)
    pre[:, 136:144, :] = jnp.zeros((5, 8, D), f32)
    row, col = lax.axis_index("rows"), lax.axis_index("cols")
    lower = row == 1
    on_left = col < 4
    w_x = w_in[:, :D]
    for step, block in enumerate(blocks):
        place_rows(pre, block, w_x, (col & 3) ^ step)
    zero = jnp.zeros((1, D), f32)
    for q in range(5):
        pre[q, 7:8, :] = jnp.where(on_left, half_pre[q, 135:136, :], zero)
        pre[q, 136:137, :] = jnp.where(on_left, zero, half_pre[q, 8:9, :])
    taps, bias = direction_taps(conv_w, lower), conv_b[...]
    for q in range(4):
        for j, part in enumerate(filter_row(pre, 5, q + 1, 128, shifted.at[q % 2], taps, bias)):
            mixed[q, 128 + TW * j : 128 + TW * (j + 1), :] = part
    tile = lax.broadcasted_iota(jnp.int32, (16, D), 0)
    low_place, high_place = jnp.where(on_left, 16, 0), jnp.where(on_left, 15, 16)
    for q in range(4):
        total = bias
        for a in range(3):
            if q + a < 5:
                at_left = (half_pre[q + a, 134:135, :], half_pre[q + a, 135:136, :], pre[q + a, 8:9, :])
                at_right = (pre[q + a, 135:136, :], half_pre[q + a, 8:9, :], half_pre[q + a, 9:10, :])
                for b in range(3):
                    total = total + taps[a][b] * jnp.where(on_left, at_left[b], at_right[b])
        value = silu(total)
        mixed[q, 16:112, :] = half_mixed[q, 16:112, :]
        for start, place in ((0, low_place), (112, high_place)):
            held = half_mixed[q, start : start + 16, :].astype(f32)
            mixed[q, start : start + 16, :] = jnp.where(tile == place, value, held).astype(bf16)

    lane = lax.broadcasted_iota(jnp.int32, (1, 128), 1)
    raw = []
    for q in range(4):
        result = dot_t(mixed[q], w_step[...])
        row_raw = result[0:TW]
        for j in range(1, 8):
            row_raw = jnp.where(lane // NH == j, result[TW * j : TW * (j + 1)], row_raw)
        raw.append(row_raw)
        attended[q] = (dot_t(reads_in[q], mixed[q]) * keep[...]).astype(bf16)
    raw = jnp.concatenate(raw, axis=0)
    left, right = lanes[2:3, :], lanes[3:4, :]
    steps = softplus(raw + lanes[0:1, :]) * (left + right)
    logs = -steps * lanes[1:2, :]
    reach = dot_wide(wide_dot(ordered[2], logs), nearer[...])
    reach = reach + wide_dot(ordered[0], logs * left) + wide_dot(ordered[1], logs * right)
    weight = split(jnp.exp(reach) * steps)
    for j in range(8):
        mask = pick[112 - NH * j : 240 - NH * j, :]
        factor = dot(weight[0], mask) + dot(weight[1], mask)
        for q in range(4):
            cells = slice(TW * j, TW * (j + 1))
            scaled[q, cells, :] = (mixed[q, cells, :].astype(f32) * factor[q * TW : (q + 1) * TW]).astype(bf16)
    finish(lower, attended, 1, scaled, base_in, gate_in, edge_in, gain, w_out, out)


def shards(feats, w_in, conv_w, conv_b, w_proj, dt_bias, a_rate, d_skip, norm_gain, w_out):
    nb = lax.axis_size("cols")
    direct = nb == 8
    vmem, hbm = pl.BlockSpec(memory_space=pltpu.VMEM), pl.BlockSpec(memory_space=pltpu.HBM)

    def shape(*dims, dtype=f32):
        return jax.ShapeDtypeStruct(dims, dtype)

    def limit(mib):
        return pltpu.CompilerParams(vmem_limit_bytes=mib << 20)

    partner = lax.ppermute(feats, "rows", [(0, 1), (1, 0)])
    params = [w_in, conv_w, conv_b[None], jnp.swapaxes(w_proj, 1, 2), dt_bias, a_rate, d_skip, norm_gain[None], w_out]
    loaded, *params = pl.pallas_call(
        load,
        out_shape=(shape(HALO, D, dtype=bf16), *[shape(*part.shape, dtype=part.dtype) for part in params]),
        in_specs=[hbm] * 10,
        out_specs=(vmem,) * 10,
        scratch_shapes=[pltpu.SemaphoreType.DMA((13,))],
        compiler_params=limit(8),
    )(*[pltpu.with_memory_space_constraint(part, pltpu.HBM) for part in (feats, *params)])
    w_in, conv_w, conv_b, w_proj, dt_bias, a_rate, d_skip, norm_gain, w_out = params
    sent, short, far = pl.pallas_call(
        pack,
        out_shape=tuple(shape(count, D, dtype=bf16) for count in (HALO, 160, 96)),
        in_specs=[vmem] * 2,
        out_specs=(vmem,) * 3,
        input_output_aliases={0: 0},
        compiler_params=limit(4),
    )(loaded, partner)
    if direct:

        def across(part, step):
            return lax.ppermute(part, "cols", [(i, i ^ step) for i in range(nb)])

        blocks = [sent] + [None] * 7
        for block in START_ORDER:
            source = FORWARDED.get(block)
            own = short if block in (2, 4) else sent
            blocks[block] = across(own, block) if source is None else across(blocks[source], block ^ source)
        sides = [blocks[1], blocks[3], blocks[7]]
    else:
        blocks = sides = [lax.all_gather(sent, "cols")]
    outs = [
        shape(8, TW, D),
        shape(128, D),
        shape(3, TW, NH * TW),
        shape(NH, NH * TW, dtype=bf16),
        shape(NH, TW, D, dtype=bf16),
        shape(256, 128, dtype=bf16),
        shape(128, 256),
        shape(128, 512, dtype=bf16),
        shape(128, 512, dtype=bf16),
    ]
    if direct:
        outs += [
            shape(3, 128, 128, dtype=bf16),
            shape(128, 128, dtype=bf16),
            shape(2 * TW, 256),
            shape(240, D, dtype=bf16),
            shape(128, D, dtype=bf16),
            shape(8, 128),
        ]
    strip_pre, gate, *masks = pl.pallas_call(
        ahead,
        out_shape=tuple(outs),
        in_specs=[vmem] * 6,
        out_specs=(vmem,) * len(outs),
        compiler_params=limit(8),
        cost_estimate=pl.CostEstimate(flops=200_000_000, bytes_accessed=1_500_000, transcendentals=50_000),
    )(sent, far, w_in, w_proj, dt_bias, a_rate)
    kept = pl.pallas_call(
        functools.partial(local, nb, len(sides)),
        out_shape=(shape(128, D), shape(4, 2 * TW, D, dtype=bf16), shape(2, 128, D)),
        in_specs=[vmem] * (15 + len(sides)),
        out_specs=(vmem,) * 3,
        scratch_shapes=[pltpu.VMEM((8, 48, D), f32), pltpu.VMEM((2, 2, 48, D), f32)],
        compiler_params=limit(16 if direct else 32),
        cost_estimate=pl.CostEstimate(flops=1_000_000_000, bytes_accessed=4_000_000, transcendentals=1_000_000),
    )(*sides, w_in, conv_w, conv_b, w_proj, dt_bias, a_rate, d_skip, strip_pre, *masks[:7])
    kept = [*kept, gate]
    tail = [w_in, conv_w, conv_b, w_proj, dt_bias, a_rate, norm_gain, w_out]
    if direct:
        half = pl.pallas_call(
            early,
            out_shape=(shape(5, 144, D), shape(4, 128, D, dtype=bf16)),
            in_specs=[vmem] * 7,
            out_specs=(vmem,) * 2,
            scratch_shapes=[pltpu.VMEM((2, 2, 144, D), f32)],
            compiler_params=limit(8),
            cost_estimate=pl.CostEstimate(flops=200_000_000, bytes_accessed=1_500_000, transcendentals=200_000),
        )(*blocks[:4], w_in, conv_w, conv_b)
        operands = [*blocks[4:], *half, *kept, *masks[7:], *tail]
        body = late
        scratch = [
            pltpu.VMEM((5, 144, D), f32),
            pltpu.VMEM((4, 256, D), bf16),
            pltpu.VMEM((4, 2 * TW, 256), bf16),
            pltpu.VMEM((4, 256, D), bf16),
            pltpu.VMEM((2, 2, 144, D), f32),
        ]
    else:
        operands = [*blocks, *kept, *tail]
        body = functools.partial(final, nb, True)
        scratch = [
            pltpu.VMEM((5, nb * TW + 16, D), f32),
            pltpu.VMEM((nb, 128, D), bf16),
            pltpu.VMEM((nb // 8, 128, 128), f32),
            pltpu.VMEM((nb // 8, 128, 128), f32),
            pltpu.VMEM((nb // 8, 128, 128), f32),
            pltpu.VMEM((4, nb * TW, 2 * TW), bf16),
            pltpu.VMEM((4, nb * TW, D), bf16),
        ]
    return pl.pallas_call(
        body,
        out_shape=shape(TH, TW, D, dtype=bf16),
        in_specs=[vmem] * len(operands),
        out_specs=vmem,
        scratch_shapes=scratch,
        compiler_params=limit(16 if direct else 48),
        cost_estimate=pl.CostEstimate(flops=1_000_000_000, bytes_accessed=4_000_000, transcendentals=1_000_000),
    )(*operands)


def solution(mesh):
    in_specs = (P(("groups", "rows"), "cols", None), P(), P(), P(), P(), P(), P(), P(), P(), P())
    out_specs = P(("groups", "rows"), "cols", None)
    return jax.shard_map(shards, mesh=mesh, in_specs=in_specs, out_specs=out_specs, check_vma=False)
```

```python
import functools

import jax
import jax.numpy as jnp
from jax import lax
from jax.experimental import pallas as pl
from jax.experimental.pallas import tpu as pltpu
from jax.sharding import PartitionSpec as P

norm_eps = 1e-05
f32, bf16 = jnp.float32, jnp.bfloat16
TH, TW, D, NH, NS = 4, 32, 256, 16, 64
START_ORDER = (6, 4, 3, 1, 2, 7, 5)
FORWARDED = {7: 6, 5: 4}
HALO = 176


def dot(a, b):
    return jnp.dot(a, b, preferred_element_type=f32)


def dot_t(a, b):
    return lax.dot_general(a, b, (((1,), (1,)), ((), ())), preferred_element_type=f32)


def split(a):
    high = a.astype(bf16)
    return high, (a - high.astype(f32)).astype(bf16)


def dot_wide(a, mask):
    high, low = split(a)
    return dot(high, mask) + dot(low, mask)


def wide_dot(mask, b):
    high, low = split(b)
    return dot(mask, high) + dot(mask, low)


def softplus(x):
    return jnp.maximum(x, 0.0) + jnp.log1p(jnp.exp(-jnp.abs(x)))


def silu(x):
    return x * jax.nn.sigmoid(x)


def iotas(rows, lanes):
    return (
        lax.broadcasted_iota(jnp.int32, (rows, lanes), 0),
        lax.broadcasted_iota(jnp.int32, (rows, lanes), 1),
    )


def ones_where(mask):
    return jnp.where(mask, 1.0, 0.0).astype(bf16)


def at(g, j):
    start = g * (8 * TW) + TW * j
    return pl.ds(start if isinstance(start, int) else pl.multiple_of(start, TW), TW)


def each(count, body):
    if count == 1:
        body(0)
    else:
        lax.fori_loop(0, count, lambda i, carry: (body(i), carry)[1], 0)


def load(feats, sent, sems):
    lower = lax.axis_index("rows") == 1
    copies = [
        pltpu.make_async_copy(
            feats.at[jnp.where(lower, i, 3 - i)], sent.at[pl.ds(TW * (i + 1), TW), :], sems.at[i]
        )
        for i in range(4)
    ]
    for copy in copies:
        copy.start()
    for copy in copies:
        copy.wait()


def load_weights(*refs):
    sources, targets, sems = refs[:9], refs[9:18], refs[18]
    copies = [
        pltpu.make_async_copy(source, target, sems.at[i]) for i, (source, target) in enumerate(zip(sources, targets))
    ]
    for copy in copies:
        copy.start()
    for copy in copies:
        copy.wait()


def pack(loaded, partner, sent, short, far):
    lower = lax.axis_index("rows") == 1
    own = [loaded[TW * (i + 1) : TW * (i + 2), :] for i in range(4)]
    rows = [partner[jnp.where(lower, i, 3 - i)] for i in range(4)] + own
    for i in range(3, 8):
        sent[TW * (i - 3) : TW * (i - 2), :] = rows[i]
        short[TW * (i - 3) : TW * (i - 2), :] = rows[i]
    for i in range(3):
        far[i * TW : (i + 1) * TW, :] = rows[i]
    wide = [part.astype(f32) for part in rows]
    edges = [part[:1] for part in wide] + [part[TW - 1 :] for part in wide]
    sent[160:HALO, :] = jnp.concatenate(edges, axis=0).astype(bf16)


def direction_taps(conv_w, lower):
    return [
        [
            jnp.where(lower, conv_w[3 * a + b : 3 * a + b + 1, :], conv_w[3 * (2 - a) + b : 3 * (2 - a) + b + 1, :])
            for b in range(3)
        ]
        for a in range(3)
    ]


def filtered(ref, count, q, base, taps, bias):
    total = jnp.broadcast_to(bias, (TW, D))
    for a in range(3):
        if 0 <= q + a - 1 < count:
            if not isinstance(base, int):
                cells = ref[q + a - 1, pl.ds(pl.multiple_of(base - 8, 8), TW + 16), :]
            for b in range(3):
                if isinstance(base, int):
                    value = ref[q + a - 1, base + b - 1 : base + b - 1 + TW, :]
                else:
                    value = cells[7 + b : 7 + b + TW]
                total = total + taps[a][b] * value
    return silu(total).astype(bf16)


def filter_row(ref, count, q, columns, shifted, taps, bias):
    def total(b, start, size):
        rows = [a for a in range(3) if 0 <= q + a - 1 < count]
        parts = [taps[a][b] * ref[q + a - 1, start : start + size, :] for a in rows]
        return functools.reduce(jnp.add, parts)

    for start in range(0, columns + 8, TW):
        size = min(TW, columns + 8 - start)
        shifted[0, start : start + size, :] = total(0, start, size)
        shifted[1, start + 8 : start + 8 + size, :] = total(2, start + 8, size)
    out = []
    for start in range(8, columns + 8, TW):
        moved = shifted[0, start - 1 : start - 1 + TW, :] + shifted[1, start + 1 : start + 1 + TW, :]
        out.append(silu(moved + (total(1, start, TW) + bias)).astype(bf16))
    return out


def ahead(nb, sent, far, w_in, w_proj, dt_bias, a_rate, *refs):
    arrived, outs = (refs[:1], refs[1:]) if nb == 8 else ((), refs)
    strip_pre, gate_out, triangle, spread_out, heads_out, select_out, same_out, walk_in, walk_out, row_masks, pick = outs[:11]
    col = lax.axis_index("cols")
    w_x = w_in[:, :D]
    far_pre = dot(far[...], w_x).astype(bf16).astype(f32)
    own_pre = dot(sent[0:160, :], w_x).astype(bf16).astype(f32)
    for i in range(8):
        strip_pre[i] = far_pre[i * TW : (i + 1) * TW] if i < 3 else own_pre[(i - 3) * TW : (i - 2) * TW]
    gate_out[...] = silu(dot(sent[TW:160, :], w_in[:, D:]))
    inner_u, inner_s = iotas(TW, NH * TW)
    inner_s = inner_s % TW
    for i, mask in enumerate((inner_u > inner_s, inner_u < inner_s, inner_u == inner_s)):
        triangle[i] = jnp.where(mask, 1.0, 0.0)
    pair_r, pair_c = iotas(NH, NH * TW)
    spread_out[...] = ones_where(pair_c // TW == pair_r)
    feature = iotas(TW, D)[1] // NH
    for h in range(NH):
        heads_out[h] = ones_where(feature == h)
    source_r, source_c = iotas(256, 128)
    select_out[...] = ones_where(source_r // TW == source_c // NH)
    t_r, s_c = iotas(128, 256)
    same_out[...] = jnp.where((t_r % TW) == (s_c % TW), 1.0, 0.0)
    walk_r, walk_c = iotas(128, 512)
    step, source, time = walk_r // NH, (walk_c % 128) // NH, walk_c // 128 + 4
    same_head = walk_r % NH == walk_c % NH
    walk_in[...] = ones_where(same_head & (source < step) & (step <= time))
    walk_out[...] = ones_where(same_head & (time <= step) & (step < source))
    tok_r, tok_c = iotas(128, 128)
    same_row = tok_r // TW == tok_c // TW
    row_masks[0] = ones_where(same_row & (tok_c <= tok_r))
    row_masks[1] = ones_where(same_row & (tok_c >= tok_r))
    pick[0:112, :] = jnp.zeros((112, D), bf16)
    pick[112:128, :] = ones_where(iotas(NH, D)[1] // NH == iotas(NH, D)[0])
    pick[128:240, :] = jnp.zeros((112, D), bf16)
    if len(outs) == 11:
        return
    ordered, nearer_out, keep_out, w_step, lanes, arrived_pre = outs[11:]
    for i, block in enumerate(arrived):
        arrived_pre[i] = dot(block[0:160, :], w_x).astype(bf16).astype(f32).reshape(5, TW, D)
    turn = jnp.where(col < 4, 0, 4)
    ordered[:, 0:128] = ones_where(same_row & (tok_c > tok_r))
    ordered[:, 128:256] = ones_where(same_row & (tok_c < tok_r))
    ordered[:, 256:384] = ones_where(same_row)
    source, target = (tok_r // NH) ^ turn, (tok_c // NH) ^ turn
    nearer = ((source > target) & (source < col)) | ((source < target) & (source > col))
    nearer_out[...] = ones_where(nearer & (tok_r % NH == tok_c % NH))
    side, block = iotas(2 * TW, 256)
    block = (block // TW) ^ turn
    keep_out[...] = jnp.where(side < TW, jnp.where(block < col, 1.0, 0.0), jnp.where(block > col, 1.0, 0.0))
    w_step[...] = jnp.concatenate(
        [jnp.where((j ^ turn) < col, w_proj[0, 0:NH, :], w_proj[1, 0:NH, :]) for j in range(8)], axis=0
    )
    lane = lax.broadcasted_iota(jnp.int32, (1, 128), 1)
    group = (lane // NH) ^ turn
    head_lane = ones_where(iotas(NH, 128)[1] % NH == iotas(NH, 128)[0])
    bias, rate = dot_wide(dt_bias[0:2, :], head_lane), dot_wide(a_rate[0:2, :], head_lane)
    lanes[0:1, :] = jnp.where(group < col, bias[0:1], bias[1:2])
    lanes[1:2, :] = jnp.where(group < col, rate[0:1], rate[1:2])
    lanes[2:3, :] = jnp.where(group < col, 1.0, 0.0)
    lanes[3:4, :] = jnp.where(group > col, 1.0, 0.0)


def local(nb, count, *refs):
    sides, refs = refs[:count], refs[count:]
    w_in, conv_w, conv_b, w_proj, dt_bias, a_rate, d_skip = refs[:7]
    strip_pre, triangle, spread, heads, select, same_col, walk_in, walk_out, row_masks, pick = refs[7:17]
    base_out, reads_out, edge_out, strip, shifted = refs[17:]
    row, col = lax.axis_index("rows"), lax.axis_index("cols")
    lower = row == 1
    w_x = w_in[:, :D]

    def pre_conv(tokens):
        return dot(tokens, w_x).astype(bf16).astype(f32)

    if count == 1:
        left = sides[0][jnp.maximum(col - 1, 0), 160:HALO, :]
        right = sides[0][jnp.minimum(col + 1, nb - 1), 160:HALO, :]
    else:
        near, further, furthest = (side[160:HALO, :] for side in sides)
        odd = lax.rem(col, 2) == 1
        left = jnp.where(odd, near, jnp.where(col == 4, furthest, further))
        right = jnp.where(odd, jnp.where(col == 3, furthest, further), near)
    left = pre_conv(left) * jnp.where(col > 0, 1.0, 0.0)
    right = pre_conv(right) * jnp.where(col < nb - 1, 1.0, 0.0)
    strip[:, 0:8, :] = jnp.zeros((8, 8, D), f32)
    strip[:, 40:48, :] = jnp.zeros((8, 8, D), f32)
    for i in range(8):
        strip[i, 8:40, :] = strip_pre[i]
        strip[i, 7:8, :] = left[8 + i : 9 + i]
        strip[i, 40:41, :] = right[i : i + 1]
    taps, bias = direction_taps(conv_w, lower), conv_b[...]
    strip_mixed = [filter_row(strip, 8, q, TW, shifted.at[q % 2], taps, bias)[0] for q in range(8)]
    own = jnp.concatenate(strip_mixed[4:], axis=0)
    column_tokens = jnp.concatenate(strip_mixed, axis=0)

    head_lane = ones_where(iotas(NH, 128)[1] % NH == iotas(NH, 128)[0])
    expand = ones_where(iotas(NH, D)[1] // NH == iotas(NH, D)[0])
    k_in = jnp.where(lower, 2, 3)
    k_out = jnp.where(lower, 3, 2)

    def pick_row(ref, k):
        return jnp.where(k == 2, ref[2:3, :], ref[3:4, :])

    lane = lax.broadcasted_iota(jnp.int32, (1, 128), 1) // NH
    head_rows = [dot_wide(pick_row(ref, k), head_lane) for ref in (dt_bias, a_rate) for k in (k_in, k_out)]

    def dense_steps(tokens, k, first, bias):
        result = dot_t(tokens, jnp.concatenate([w_proj[k, 0:NH, :]] * 8, axis=0))
        raw = result[0:TW]
        for s in range(first + 1, 8):
            raw = jnp.where(lane == s, result[(s - first) * TW : (s - first + 1) * TW], raw)
        return softplus(raw + bias)

    steps_in = dense_steps(column_tokens, k_in, 0, head_rows[0])
    steps_out = dense_steps(own, k_out, 4, head_rows[1])
    gap = dot(jnp.concatenate(split(-steps_in * head_rows[2]), axis=0), walk_in[...])
    gap_out = dot(jnp.concatenate(split(-steps_out * head_rows[3]), axis=0), walk_out[...])
    gap = (gap[:TW] + gap[TW:]) + (gap_out[:TW] + gap_out[TW:])
    decay = jnp.exp(gap)
    write_in = dot_t(column_tokens, w_proj[k_in, NH : NH + NS, :]).astype(bf16)
    write_out = dot_t(own, w_proj[k_out, NH : NH + NS, :]).astype(bf16)
    read_in = dot_t(own, w_proj[k_in, NH + NS :, :]).astype(bf16)
    read_out = dot_t(own, w_proj[k_out, NH + NS :, :]).astype(bf16)
    scores_in = dot((dot_t(read_in, write_in) * same_col[...]).astype(bf16), select[...])
    scores_out = dot((dot_t(read_out, write_out) * same_col[:, :128]).astype(bf16), select[128:, :])
    vertical_weights = []
    for t in range(4):
        rows = slice(t * TW, (t + 1) * TW)
        sum_in = scores_in[rows] * (steps_in * jnp.where(lane <= t + 4, 1.0, 0.0))
        sum_out = scores_out[rows] * (steps_out * jnp.where(lane >= t + 4, 1.0, 0.0))
        vertical_weights.append((sum_in + sum_out) * decay[:, t * 128 : (t + 1) * 128])
    vertical_weights = jnp.concatenate(vertical_weights, axis=0).astype(bf16)
    projected = [dot_t(own, w_proj[k]) for k in range(2)]
    steps = [softplus(projected[k][:, :NH] + dt_bias[k : k + 1, :]) for k in range(2)]
    logs = [-steps[k] * a_rate[k : k + 1, :] for k in range(2)]
    write = [projected[k][:, NH : NH + NS].astype(bf16) for k in range(2)]
    read = [projected[k][:, NH + NS :].astype(bf16) for k in range(2)]
    reach = [dot(read[k], w_proj[k, NH : NH + NS, :]).astype(bf16) for k in range(2)]
    for k in range(2):
        edge_out[k] = dot(jnp.exp(wide_dot(row_masks[k], logs[k])).astype(bf16), expand)
    stacked = [part for k in range(2) for part in split(logs[k])] + [steps[k].astype(bf16) for k in range(2)]
    wide = dot(jnp.concatenate(stacked, axis=0), spread[...])
    wide = [wide[i * 128 : (i + 1) * 128] for i in range(6)]
    later, sooner, equal = triangle[0], triangle[1], triangle[2]
    time_r, time_c = iotas(TW, TW)
    first, second = ones_where(time_c <= time_r), ones_where(time_c >= time_r)
    walk = jnp.concatenate([first, first, second, second], axis=1)
    allowed = (later + equal, sooner + equal)
    across = []
    for q in range(4):
        rows = slice(q * TW, (q + 1) * TW)
        parts = [(wide[i][rows] * (later if i < 2 else sooner)).astype(bf16) for i in range(4)]
        gaps = dot(walk, jnp.concatenate(parts, axis=0))
        weights = jnp.zeros((TW, NH * TW), f32)
        for k, keep in enumerate(allowed):
            scores = dot_t(read[k][rows], jnp.concatenate([write[k][rows]] * NH, axis=0))
            step_row = jnp.sum(wide[4 + k][rows] * equal, axis=0, keepdims=True)
            weights = weights + scores * step_row * keep
        weights = (weights * jnp.exp(gaps)).astype(bf16)
        values = own[rows]
        spread_values = jnp.concatenate(
            [values * heads[h] for h in range(NH)], axis=0
        )
        result = dot(weights, spread_values)
        reads_out[q] = jnp.concatenate([reach[0][rows], reach[1][rows]], axis=0)
        across.append(result)
    across = jnp.concatenate(across, axis=0)

    skips = dot_wide(d_skip[...], expand)
    own_wide = own.astype(f32)
    vertical = (skips[2:3] + skips[3:4]) * own_wide
    for s in range(8):
        factor = dot(vertical_weights, pick[112 - NH * s : 240 - NH * s, :])
        values = strip_mixed[s].astype(f32)
        vertical = vertical + factor * jnp.concatenate([values] * 4, axis=0)
    base_out[...] = across + (skips[0:1] + skips[1:2]) * own_wide + vertical.astype(bf16).astype(f32)


def final(nb, gathered, *refs):
    count = 1 if gathered else nb
    blocks, refs = refs[:count], refs[count:]
    base_in, reads_in, edge_in, gate_in = refs[:4]
    w_in, conv_w, conv_b, w_proj, dt_bias, a_rate, gain, w_out, out = refs[4:13]
    pre, mixed, la_all, dt_all, totals, attended, scaled = refs[13:]
    row, col = lax.axis_index("rows"), lax.axis_index("cols")
    lower = row == 1
    ng = nb // 8
    w_x = w_in[:, :D]

    def pre_conv(tokens):
        return dot(tokens, w_x).astype(bf16).astype(f32)

    pre[:, 0:8, :] = jnp.zeros((5, 8, D), f32)
    pre[:, 8 + nb * TW :, :] = jnp.zeros((5, 8, D), f32)

    def place_block(tokens, position):
        rows = pre_conv(tokens)
        base = pl.multiple_of(position * TW + 8, 8)
        for q in range(5):
            pre[q, pl.ds(base, TW), :] = rows[q * TW : (q + 1) * TW]

    if gathered:
        each(nb, lambda j: place_block(blocks[0][j, 0:160, :], j))
    else:
        for step in range(nb):
            place_block(blocks[step][0:160, :], col ^ step)
    taps, bias = direction_taps(conv_w, lower), conv_b[...]

    head_lane = ones_where(iotas(NH, 128)[1] % NH == iotas(NH, 128)[0])
    tok_r, tok_c = iotas(128, 128)
    same_row = tok_r // TW == tok_c // TW
    after = ones_where(same_row & (tok_c > tok_r))
    before = ones_where(same_row & (tok_c < tok_r))
    row_ones = ones_where(same_row)
    lane = lax.broadcasted_iota(jnp.int32, (1, 128), 1)
    bias_2 = dot_wide(dt_bias[0:2, :], head_lane)
    rate_2 = dot_wide(a_rate[0:2, :], head_lane)

    def first_pass(g):
        group = lane // NH + g * 8
        is_left = group < col
        w_step = jnp.concatenate(
            [jnp.where(g * 8 + j < col, w_proj[0, 0:NH, :], w_proj[1, 0:NH, :]) for j in range(8)], axis=0
        )
        raw = jnp.zeros((128, 128), f32)
        for j in range(8):
            base = g * (8 * TW) + (8 + TW * j)
            for q in range(1, 5):
                mixed[g * 8 + j, (q - 1) * TW : q * TW, :] = filtered(pre, 5, q, base, taps, bias)
            raw = jnp.where(lane // NH == j, dot_t(mixed[g * 8 + j], w_step), raw)
            block = g * 8 + j
            side = lax.broadcasted_iota(jnp.int32, (1, 2 * TW), 1) < TW
            keep = jnp.where(side, jnp.where(block < col, 1.0, 0.0), jnp.where(block > col, 1.0, 0.0))
            for q in range(4):
                tokens = mixed[g * 8 + j, q * TW : (q + 1) * TW, :]
                attended[q, at(g, j), :] = (dot_t(tokens, reads_in[q]) * keep).astype(bf16)
        steps = softplus(raw + jnp.where(is_left, bias_2[0:1], bias_2[1:2]))
        steps = jnp.where(group == col, 0.0, steps)
        logs = -steps * jnp.where(is_left, rate_2[0:1], rate_2[1:2])
        dt_all[g] = steps
        la_all[g] = logs
        totals[g] = wide_dot(row_ones, logs)

    each(ng, first_pass)

    both_ways = jnp.concatenate([after, before], axis=1)

    def second_pass(g):
        group = lane // NH + g * 8
        logs = la_all[g]
        stacked = jnp.concatenate([jnp.where(group < col, logs, 0.0), jnp.where(group > col, logs, 0.0)], axis=0)
        reach = wide_dot(both_ways, stacked)

        def add_group(other, total):
            source, target = other * 8 + tok_r // NH, g * 8 + tok_c // NH
            nearer = ((source > target) & (source < col)) | ((source < target) & (source > col))
            nearer = nearer & (tok_r % NH == tok_c % NH)
            return total + dot_wide(totals[other], ones_where(nearer))

        if ng == 1:
            reach = add_group(0, reach)
        else:
            reach = lax.fori_loop(0, ng, add_group, reach)
        weight = jnp.concatenate(split(jnp.exp(reach) * dt_all[g]), axis=1)
        expand_r, expand_c = iotas(256, D)
        for j in range(8):
            pick = ones_where((expand_r % 128) == j * NH + expand_c // NH)
            factor = dot(weight, pick)
            values = (mixed[g * 8 + j].astype(f32) * factor).astype(bf16)
            for q in range(4):
                scaled[q, at(g, j), :] = values[q * TW : (q + 1) * TW]

    each(ng, second_pass)

    finish(lower, attended, 0, scaled, base_in, gate_in, edge_in, gain, w_out, out)


def finish(lower, attended, axis, scaled, base_in, gate_in, edge_in, gain, w_out, out):
    entered = []
    for q in range(4):
        rows = slice(q * TW, (q + 1) * TW)
        both = lax.dot_general(attended[q], scaled[q], (((axis,), (0,)), ((), ())), preferred_element_type=f32)
        entered.append(both[:TW] * edge_in[0, rows, :] + both[TW:] * edge_in[1, rows, :])
    combined = base_in[...] + jnp.concatenate(entered, axis=0)

    centre = combined - jnp.mean(combined, axis=-1, keepdims=True)
    normed = centre * lax.rsqrt(jnp.mean(centre * centre, axis=-1, keepdims=True) + norm_eps) * gain[...]
    gated = (normed * gate_in[...]).astype(bf16)
    result = dot(gated, w_out[...]).astype(bf16)
    for i in range(4):
        out[jnp.where(lower, i, 3 - i)] = result[i * TW : (i + 1) * TW]


def early(strip_pre, first, second, third, w_in, conv_w, conv_b, pre, mixed, shifted):
    col = lax.axis_index("cols")
    lower = lax.axis_index("rows") == 1
    w_x = w_in[:, :D]
    pre[:, 0:8, :] = jnp.zeros((5, 8, D), f32)
    pre[:, 136:144, :] = jnp.zeros((5, 8, D), f32)
    for step, block in ((1, first), (2, second), (3, third)):
        place_rows(pre, block, w_x, (col & 3) ^ step)
    base = pl.multiple_of((col & 3) * TW + 8, 8)
    for q in range(5):
        pre[q, pl.ds(base, TW), :] = strip_pre[3 + q]
    taps, bias = direction_taps(conv_w, lower), conv_b[...]
    for q in range(1, 5):
        for j, part in enumerate(filter_row(pre, 5, q, 128, shifted.at[q % 2], taps, bias)):
            mixed[q - 1, TW * j : TW * (j + 1), :] = part


def place_rows(pre, block, w_x, position):
    rows = dot(block[0:160, :], w_x).astype(bf16).astype(f32)
    base = pl.multiple_of(position * TW + 8, 8)
    for q in range(5):
        pre[q, pl.ds(base, TW), :] = rows[q * TW : (q + 1) * TW]


def late(*refs):
    blocks, arrived_pre, refs = (refs[0], refs[1], refs[3]), refs[2], refs[4:]
    (half_pre, half_mixed, base_in, reads_in, edge_in, gate_in), refs = refs[:6], refs[6:]
    pick, ordered, nearer, keep, w_step, lanes = refs[:6]
    refs = refs[6:]
    w_in, conv_w, conv_b, _, _, _, gain, w_out, out = refs[:9]
    pre, mixed, attended, scaled, shifted = refs[9:]
    pre[:, 0:8, :] = jnp.zeros((5, 8, D), f32)
    pre[:, 136:144, :] = jnp.zeros((5, 8, D), f32)
    row, col = lax.axis_index("rows"), lax.axis_index("cols")
    lower = row == 1
    on_left = col < 4
    w_x = w_in[:, :D]
    for step, block in zip((0, 1, 3), blocks):
        place_rows(pre, block, w_x, (col & 3) ^ step)
    base = pl.multiple_of(((col & 3) ^ 2) * TW + 8, 8)
    for q in range(5):
        pre[q, pl.ds(base, TW), :] = arrived_pre[0, q]
    zero = jnp.zeros((1, D), f32)
    for q in range(5):
        pre[q, 7:8, :] = jnp.where(on_left, half_pre[q, 135:136, :], zero)
        pre[q, 136:137, :] = jnp.where(on_left, zero, half_pre[q, 8:9, :])
    taps, bias = direction_taps(conv_w, lower), conv_b[...]
    for q in range(4):
        for j, part in enumerate(filter_row(pre, 5, q + 1, 128, shifted.at[q % 2], taps, bias)):
            mixed[q, 128 + TW * j : 128 + TW * (j + 1), :] = part
    tile = lax.broadcasted_iota(jnp.int32, (16, D), 0)
    low_place, high_place = jnp.where(on_left, 16, 0), jnp.where(on_left, 15, 16)
    for q in range(4):
        total = bias
        for a in range(3):
            if q + a < 5:
                at_left = (half_pre[q + a, 134:135, :], half_pre[q + a, 135:136, :], pre[q + a, 8:9, :])
                at_right = (pre[q + a, 135:136, :], half_pre[q + a, 8:9, :], half_pre[q + a, 9:10, :])
                for b in range(3):
                    total = total + taps[a][b] * jnp.where(on_left, at_left[b], at_right[b])
        value = silu(total)
        mixed[q, 16:112, :] = half_mixed[q, 16:112, :]
        for start, place in ((0, low_place), (112, high_place)):
            held = half_mixed[q, start : start + 16, :].astype(f32)
            mixed[q, start : start + 16, :] = jnp.where(tile == place, value, held).astype(bf16)

    lane = lax.broadcasted_iota(jnp.int32, (1, 128), 1)
    raw = []
    for q in range(4):
        result = dot_t(mixed[q], w_step[...])
        row_raw = result[0:TW]
        for j in range(1, 8):
            row_raw = jnp.where(lane // NH == j, result[TW * j : TW * (j + 1)], row_raw)
        raw.append(row_raw)
        attended[q] = (dot_t(reads_in[q], mixed[q]) * keep[...]).astype(bf16)
    raw = jnp.concatenate(raw, axis=0)
    left, right = lanes[2:3, :], lanes[3:4, :]
    steps = softplus(raw + lanes[0:1, :]) * (left + right)
    logs = -steps * lanes[1:2, :]
    stacked = jnp.concatenate([logs * left, logs * right, dot_wide(logs, nearer[...])], axis=0)
    reach = wide_dot(ordered[...], stacked)
    weight = split(jnp.exp(reach) * steps)
    for j in range(8):
        mask = pick[112 - NH * j : 240 - NH * j, :]
        factor = dot(weight[0], mask)
        for q in range(4):
            cells = slice(TW * j, TW * (j + 1))
            scaled[q, cells, :] = (mixed[q, cells, :].astype(f32) * factor[q * TW : (q + 1) * TW]).astype(bf16)
    finish(lower, attended, 1, scaled, base_in, gate_in, edge_in, gain, w_out, out)


def shards(feats, w_in, conv_w, conv_b, w_proj, dt_bias, a_rate, d_skip, norm_gain, w_out):
    nb = lax.axis_size("cols")
    direct = nb == 8
    vmem, hbm = pl.BlockSpec(memory_space=pltpu.VMEM), pl.BlockSpec(memory_space=pltpu.HBM)

    def shape(*dims, dtype=f32):
        return jax.ShapeDtypeStruct(dims, dtype)

    def limit(mib):
        return pltpu.CompilerParams(vmem_limit_bytes=mib << 20)

    partner = lax.ppermute(feats, "rows", [(0, 1), (1, 0)])
    params = [w_in, conv_w, conv_b[None], jnp.swapaxes(w_proj, 1, 2), dt_bias, a_rate, d_skip, norm_gain[None], w_out]
    loaded = pl.pallas_call(
        load,
        out_shape=shape(HALO, D, dtype=bf16),
        in_specs=[hbm],
        out_specs=vmem,
        scratch_shapes=[pltpu.SemaphoreType.DMA((4,))],
        compiler_params=limit(8),
    )(pltpu.with_memory_space_constraint(feats, pltpu.HBM))
    params = pl.pallas_call(
        load_weights,
        out_shape=tuple(shape(*part.shape, dtype=part.dtype) for part in params),
        in_specs=[hbm] * 9,
        out_specs=(vmem,) * 9,
        scratch_shapes=[pltpu.SemaphoreType.DMA((9,))],
        compiler_params=limit(8),
    )(*[pltpu.with_memory_space_constraint(part, pltpu.HBM) for part in params])
    w_in, conv_w, conv_b, w_proj, dt_bias, a_rate, d_skip, norm_gain, w_out = params
    sent, short, far = pl.pallas_call(
        pack,
        out_shape=tuple(shape(count, D, dtype=bf16) for count in (HALO, 160, 96)),
        in_specs=[vmem] * 2,
        out_specs=(vmem,) * 3,
        input_output_aliases={0: 0},
        compiler_params=limit(4),
    )(loaded, partner)
    if direct:

        def across(part, step):
            return lax.ppermute(part, "cols", [(i, i ^ step) for i in range(nb)])

        blocks = [sent] + [None] * 7
        for block in START_ORDER:
            source = FORWARDED.get(block)
            own = short if block in (2, 4) else sent
            blocks[block] = across(own, block) if source is None else across(blocks[source], block ^ source)
        sides = [blocks[1], blocks[3], blocks[7]]
    else:
        blocks = sides = [lax.all_gather(sent, "cols")]
    outs = [
        shape(8, TW, D),
        shape(128, D),
        shape(3, TW, NH * TW),
        shape(NH, NH * TW, dtype=bf16),
        shape(NH, TW, D, dtype=bf16),
        shape(256, 128, dtype=bf16),
        shape(128, 256),
        shape(128, 512, dtype=bf16),
        shape(128, 512, dtype=bf16),
        shape(2, 128, 128, dtype=bf16),
        shape(240, D, dtype=bf16),
    ]
    if direct:
        outs += [
            shape(128, 384, dtype=bf16),
            shape(128, 128, dtype=bf16),
            shape(2 * TW, 256),
            shape(128, D, dtype=bf16),
            shape(8, 128),
            shape(1, 5, TW, D),
        ]
    strip_pre, gate, *masks = pl.pallas_call(
        functools.partial(ahead, nb),
        out_shape=tuple(outs),
        in_specs=[vmem] * (7 if direct else 6),
        out_specs=(vmem,) * len(outs),
        compiler_params=limit(8),
        cost_estimate=pl.CostEstimate(flops=200_000_000, bytes_accessed=1_500_000, transcendentals=50_000),
    )(sent, far, w_in, w_proj, dt_bias, a_rate, *((blocks[6],) if direct else ()))
    kept = pl.pallas_call(
        functools.partial(local, nb, len(sides)),
        out_shape=(shape(128, D), shape(4, 2 * TW, D, dtype=bf16), shape(2, 128, D)),
        in_specs=[vmem] * (17 + len(sides)),
        out_specs=(vmem,) * 3,
        scratch_shapes=[pltpu.VMEM((8, 48, D), f32), pltpu.VMEM((2, 2, 48, D), f32)],
        compiler_params=limit(16 if direct else 32),
        cost_estimate=pl.CostEstimate(flops=1_000_000_000, bytes_accessed=4_000_000, transcendentals=1_000_000),
    )(*sides, w_in, conv_w, conv_b, w_proj, dt_bias, a_rate, d_skip, strip_pre, *masks[:9])
    kept = [*kept, gate]
    tail = [w_in, conv_w, conv_b, w_proj, dt_bias, a_rate, norm_gain, w_out]
    if direct:
        half = pl.pallas_call(
            early,
            out_shape=(shape(5, 144, D), shape(4, 128, D, dtype=bf16)),
            in_specs=[vmem] * 7,
            out_specs=(vmem,) * 2,
            scratch_shapes=[pltpu.VMEM((2, 2, 144, D), f32)],
            compiler_params=limit(8),
            cost_estimate=pl.CostEstimate(flops=200_000_000, bytes_accessed=1_500_000, transcendentals=200_000),
        )(strip_pre, *blocks[1:4], w_in, conv_w, conv_b)
        operands = [*blocks[4:6], masks[-1], blocks[7], *half, *kept, *masks[8:-1], *tail]
        body = late
        scratch = [
            pltpu.VMEM((5, 144, D), f32),
            pltpu.VMEM((4, 256, D), bf16),
            pltpu.VMEM((4, 2 * TW, 256), bf16),
            pltpu.VMEM((4, 256, D), bf16),
            pltpu.VMEM((2, 2, 144, D), f32),
        ]
    else:
        operands = [*blocks, *kept, *tail]
        body = functools.partial(final, nb, True)
        scratch = [
            pltpu.VMEM((5, nb * TW + 16, D), f32),
            pltpu.VMEM((nb, 128, D), bf16),
            pltpu.VMEM((nb // 8, 128, 128), f32),
            pltpu.VMEM((nb // 8, 128, 128), f32),
            pltpu.VMEM((nb // 8, 128, 128), f32),
            pltpu.VMEM((4, nb * TW, 2 * TW), bf16),
            pltpu.VMEM((4, nb * TW, D), bf16),
        ]
    return pl.pallas_call(
        body,
        out_shape=shape(TH, TW, D, dtype=bf16),
        in_specs=[vmem] * len(operands),
        out_specs=vmem,
        scratch_shapes=scratch,
        compiler_params=limit(16 if direct else 48),
        cost_estimate=pl.CostEstimate(flops=1_000_000_000, bytes_accessed=4_000_000, transcendentals=1_000_000),
    )(*operands)


def solution(mesh):
    in_specs = (P(("groups", "rows"), "cols", None), P(), P(), P(), P(), P(), P(), P(), P(), P())
    out_specs = P(("groups", "rows"), "cols", None)
    return jax.shard_map(shards, mesh=mesh, in_specs=in_specs, out_specs=out_specs, check_vma=False)
```

```python
import functools

import jax
import jax.numpy as jnp
from jax import lax
from jax.experimental import pallas as pl
from jax.experimental.pallas import tpu as pltpu
from jax.sharding import PartitionSpec as P

norm_eps = 1e-05
f32, bf16 = jnp.float32, jnp.bfloat16
TH, TW, D, NH, NS = 4, 32, 256, 16, 64
START_ORDER = (6, 4, 3, 1, 2, 7, 5)
FORWARDED = {7: 6, 5: 4}
HALO = 176


def dot(a, b):
    return jnp.dot(a, b, preferred_element_type=f32)


def dot_t(a, b):
    return lax.dot_general(a, b, (((1,), (1,)), ((), ())), preferred_element_type=f32)


def split(a):
    high = a.astype(bf16)
    return high, (a - high.astype(f32)).astype(bf16)


def dot_wide(a, mask):
    high, low = split(a)
    return dot(high, mask) + dot(low, mask)


def wide_dot(mask, b):
    high, low = split(b)
    return dot(mask, high) + dot(mask, low)


def softplus(x):
    return jnp.maximum(x, 0.0) + jnp.log1p(jnp.exp(-jnp.abs(x)))


def silu(x):
    return x * jax.nn.sigmoid(x)


def iotas(rows, lanes):
    return (
        lax.broadcasted_iota(jnp.int32, (rows, lanes), 0),
        lax.broadcasted_iota(jnp.int32, (rows, lanes), 1),
    )


def ones_where(mask):
    return jnp.where(mask, 1.0, 0.0).astype(bf16)


def at(g, j):
    start = g * (8 * TW) + TW * j
    return pl.ds(start if isinstance(start, int) else pl.multiple_of(start, TW), TW)


def each(count, body):
    if count == 1:
        body(0)
    else:
        lax.fori_loop(0, count, lambda i, carry: (body(i), carry)[1], 0)


def load(feats, sent, sems):
    lower = lax.axis_index("rows") == 1
    copies = [
        pltpu.make_async_copy(
            feats.at[jnp.where(lower, i, 3 - i)], sent.at[pl.ds(TW * (i + 1), TW), :], sems.at[i]
        )
        for i in range(4)
    ]
    for copy in copies:
        copy.start()
    for copy in copies:
        copy.wait()


def load_weights(*refs):
    sources, targets, sems = refs[:9], refs[9:18], refs[18]
    copies = [
        pltpu.make_async_copy(source, target, sems.at[i]) for i, (source, target) in enumerate(zip(sources, targets))
    ]
    for copy in copies:
        copy.start()
    for copy in copies:
        copy.wait()


def pack(loaded, partner, sent, short, far):
    lower = lax.axis_index("rows") == 1
    own = [loaded[TW * (i + 1) : TW * (i + 2), :] for i in range(4)]
    rows = [partner[jnp.where(lower, i, 3 - i)] for i in range(4)] + own
    for i in range(3, 8):
        sent[TW * (i - 3) : TW * (i - 2), :] = rows[i]
        short[TW * (i - 3) : TW * (i - 2), :] = rows[i]
    for i in range(3):
        far[i * TW : (i + 1) * TW, :] = rows[i]
    wide = [part.astype(f32) for part in rows]
    edges = [part[:1] for part in wide] + [part[TW - 1 :] for part in wide]
    sent[160:HALO, :] = jnp.concatenate(edges, axis=0).astype(bf16)


def direction_taps(conv_w, lower):
    return [
        [
            jnp.where(lower, conv_w[3 * a + b : 3 * a + b + 1, :], conv_w[3 * (2 - a) + b : 3 * (2 - a) + b + 1, :])
            for b in range(3)
        ]
        for a in range(3)
    ]


def filtered(ref, count, q, base, taps, bias):
    total = jnp.broadcast_to(bias, (TW, D))
    for a in range(3):
        if 0 <= q + a - 1 < count:
            if not isinstance(base, int):
                cells = ref[q + a - 1, pl.ds(pl.multiple_of(base - 8, 8), TW + 16), :]
            for b in range(3):
                if isinstance(base, int):
                    value = ref[q + a - 1, base + b - 1 : base + b - 1 + TW, :]
                else:
                    value = cells[7 + b : 7 + b + TW]
                total = total + taps[a][b] * value
    return silu(total).astype(bf16)


def filter_row(ref, count, q, columns, shifted, taps, bias):
    def total(b, start, size):
        rows = [a for a in range(3) if 0 <= q + a - 1 < count]
        parts = [taps[a][b] * ref[q + a - 1, start : start + size, :] for a in rows]
        return functools.reduce(jnp.add, parts)

    for start in range(0, columns + 8, TW):
        size = min(TW, columns + 8 - start)
        shifted[0, start : start + size, :] = total(0, start, size)
        shifted[1, start + 8 : start + 8 + size, :] = total(2, start + 8, size)
    out = []
    for start in range(8, columns + 8, TW):
        moved = shifted[0, start - 1 : start - 1 + TW, :] + shifted[1, start + 1 : start + 1 + TW, :]
        out.append(silu(moved + (total(1, start, TW) + bias)).astype(bf16))
    return out


def ahead(nb, sent, far, w_in, w_proj, dt_bias, a_rate, *refs):
    arrived, outs = (refs[:1], refs[1:]) if nb == 8 else ((), refs)
    strip_pre, gate_out, triangle, spread_out, heads_out, select_out, same_out, walk_in, walk_out, row_masks, pick = outs[:11]
    col = lax.axis_index("cols")
    w_x = w_in[:, :D]
    far_pre = dot(far[...], w_x).astype(bf16).astype(f32)
    own_pre = dot(sent[0:160, :], w_x).astype(bf16).astype(f32)
    for i in range(8):
        strip_pre[i] = far_pre[i * TW : (i + 1) * TW] if i < 3 else own_pre[(i - 3) * TW : (i - 2) * TW]
    gate_out[...] = silu(dot(sent[TW:160, :], w_in[:, D:]))
    inner_u, inner_s = iotas(TW, NH * TW)
    inner_s = inner_s % TW
    for i, mask in enumerate((inner_u > inner_s, inner_u < inner_s, inner_u == inner_s)):
        triangle[i] = jnp.where(mask, 1.0, 0.0)
    pair_r, pair_c = iotas(NH, NH * TW)
    spread_out[...] = ones_where(pair_c // TW == pair_r)
    feature = iotas(TW, D)[1] // NH
    for h in range(NH):
        heads_out[h] = ones_where(feature == h)
    source_r, source_c = iotas(256, 128)
    select_out[...] = ones_where(source_r // TW == source_c // NH)
    t_r, s_c = iotas(128, 256)
    same_out[...] = jnp.where((t_r % TW) == (s_c % TW), 1.0, 0.0)
    walk_r, walk_c = iotas(128, 512)
    step, source, time = walk_r // NH, (walk_c % 128) // NH, walk_c // 128 + 4
    same_head = walk_r % NH == walk_c % NH
    walk_in[...] = ones_where(same_head & (source < step) & (step <= time))
    walk_out[...] = ones_where(same_head & (time <= step) & (step < source))
    tok_r, tok_c = iotas(128, 128)
    same_row = tok_r // TW == tok_c // TW
    row_masks[0] = ones_where(same_row & (tok_c <= tok_r))
    row_masks[1] = ones_where(same_row & (tok_c >= tok_r))
    pick[0:112, :] = jnp.zeros((112, D), bf16)
    pick[112:128, :] = ones_where(iotas(NH, D)[1] // NH == iotas(NH, D)[0])
    pick[128:240, :] = jnp.zeros((112, D), bf16)
    if len(outs) == 11:
        return
    ordered, nearer_out, keep_out, w_step, lanes, arrived_pre = outs[11:]
    for i, block in enumerate(arrived):
        arrived_pre[i] = dot(block[0:160, :], w_x).astype(bf16).astype(f32).reshape(5, TW, D)
    turn = jnp.where(col < 4, 0, 4)
    ordered[:, 0:128] = ones_where(same_row & (tok_c > tok_r))
    ordered[:, 128:256] = ones_where(same_row & (tok_c < tok_r))
    ordered[:, 256:384] = ones_where(same_row)
    source, target = (tok_r // NH) ^ turn, (tok_c // NH) ^ turn
    nearer = ((source > target) & (source < col)) | ((source < target) & (source > col))
    nearer_out[...] = ones_where(nearer & (tok_r % NH == tok_c % NH))
    side, block = iotas(2 * TW, 256)
    block = (block // TW) ^ turn
    keep_out[...] = jnp.where(side < TW, jnp.where(block < col, 1.0, 0.0), jnp.where(block > col, 1.0, 0.0))
    w_step[...] = jnp.concatenate(
        [jnp.where((j ^ turn) < col, w_proj[0, 0:NH, :], w_proj[1, 0:NH, :]) for j in range(8)], axis=0
    )
    lane = lax.broadcasted_iota(jnp.int32, (1, 128), 1)
    group = (lane // NH) ^ turn
    head_lane = ones_where(iotas(NH, 128)[1] % NH == iotas(NH, 128)[0])
    bias, rate = dot_wide(dt_bias[0:2, :], head_lane), dot_wide(a_rate[0:2, :], head_lane)
    lanes[0:1, :] = jnp.where(group < col, bias[0:1], bias[1:2])
    lanes[1:2, :] = jnp.where(group < col, rate[0:1], rate[1:2])
    lanes[2:3, :] = jnp.where(group < col, 1.0, 0.0)
    lanes[3:4, :] = jnp.where(group > col, 1.0, 0.0)


def local(nb, count, *refs):
    sides, refs = refs[:count], refs[count:]
    w_in, conv_w, conv_b, w_proj, dt_bias, a_rate, d_skip = refs[:7]
    strip_pre, triangle, spread, heads, select, same_col, walk_in, walk_out, row_masks, pick = refs[7:17]
    base_out, reads_out, edge_out, strip, shifted = refs[17:]
    row, col = lax.axis_index("rows"), lax.axis_index("cols")
    lower = row == 1
    w_x = w_in[:, :D]

    def pre_conv(tokens):
        return dot(tokens, w_x).astype(bf16).astype(f32)

    if count == 1:
        left = sides[0][jnp.maximum(col - 1, 0), 160:HALO, :]
        right = sides[0][jnp.minimum(col + 1, nb - 1), 160:HALO, :]
    else:
        near, further, furthest = (side[160:HALO, :] for side in sides)
        odd = lax.rem(col, 2) == 1
        left = jnp.where(odd, near, jnp.where(col == 4, furthest, further))
        right = jnp.where(odd, jnp.where(col == 3, furthest, further), near)
    left = pre_conv(left) * jnp.where(col > 0, 1.0, 0.0)
    right = pre_conv(right) * jnp.where(col < nb - 1, 1.0, 0.0)
    strip[:, 0:8, :] = jnp.zeros((8, 8, D), f32)
    strip[:, 40:48, :] = jnp.zeros((8, 8, D), f32)
    for i in range(8):
        strip[i, 8:40, :] = strip_pre[i]
        strip[i, 7:8, :] = left[8 + i : 9 + i]
        strip[i, 40:41, :] = right[i : i + 1]
    taps, bias = direction_taps(conv_w, lower), conv_b[...]
    strip_mixed = [filter_row(strip, 8, q, TW, shifted.at[q % 2], taps, bias)[0] for q in range(8)]
    own = jnp.concatenate(strip_mixed[4:], axis=0)
    column_tokens = jnp.concatenate(strip_mixed, axis=0)

    head_lane = ones_where(iotas(NH, 128)[1] % NH == iotas(NH, 128)[0])
    expand = ones_where(iotas(NH, D)[1] // NH == iotas(NH, D)[0])
    k_in = jnp.where(lower, 2, 3)
    k_out = jnp.where(lower, 3, 2)

    def pick_row(ref, k):
        return jnp.where(k == 2, ref[2:3, :], ref[3:4, :])

    lane = lax.broadcasted_iota(jnp.int32, (1, 128), 1) // NH
    head_rows = [dot_wide(pick_row(ref, k), head_lane) for ref in (dt_bias, a_rate) for k in (k_in, k_out)]

    def dense_steps(tokens, k, first, bias):
        result = dot_t(tokens, jnp.concatenate([w_proj[k, 0:NH, :]] * 8, axis=0))
        raw = result[0:TW]
        for s in range(first + 1, 8):
            raw = jnp.where(lane == s, result[(s - first) * TW : (s - first + 1) * TW], raw)
        return softplus(raw + bias)

    steps_in = dense_steps(column_tokens, k_in, 0, head_rows[0])
    steps_out = dense_steps(own, k_out, 4, head_rows[1])
    gap = dot(jnp.concatenate(split(-steps_in * head_rows[2]), axis=0), walk_in[...])
    gap_out = dot(jnp.concatenate(split(-steps_out * head_rows[3]), axis=0), walk_out[...])
    gap = (gap[:TW] + gap[TW:]) + (gap_out[:TW] + gap_out[TW:])
    decay = jnp.exp(gap)
    write_in = dot_t(column_tokens, w_proj[k_in, NH : NH + NS, :]).astype(bf16)
    write_out = dot_t(own, w_proj[k_out, NH : NH + NS, :]).astype(bf16)
    read_in = dot_t(own, w_proj[k_in, NH + NS :, :]).astype(bf16)
    read_out = dot_t(own, w_proj[k_out, NH + NS :, :]).astype(bf16)
    scores_in = dot((dot_t(read_in, write_in) * same_col[...]).astype(bf16), select[...])
    scores_out = dot((dot_t(read_out, write_out) * same_col[:, :128]).astype(bf16), select[128:, :])
    vertical_weights = []
    for t in range(4):
        rows = slice(t * TW, (t + 1) * TW)
        sum_in = scores_in[rows] * (steps_in * jnp.where(lane <= t + 4, 1.0, 0.0))
        sum_out = scores_out[rows] * (steps_out * jnp.where(lane >= t + 4, 1.0, 0.0))
        vertical_weights.append((sum_in + sum_out) * decay[:, t * 128 : (t + 1) * 128])
    vertical_weights = jnp.concatenate(vertical_weights, axis=0).astype(bf16)
    projected = [dot_t(own, w_proj[k]) for k in range(2)]
    steps = [softplus(projected[k][:, :NH] + dt_bias[k : k + 1, :]) for k in range(2)]
    logs = [-steps[k] * a_rate[k : k + 1, :] for k in range(2)]
    write = [projected[k][:, NH : NH + NS].astype(bf16) for k in range(2)]
    read = [projected[k][:, NH + NS :].astype(bf16) for k in range(2)]
    reach = [dot(read[k], w_proj[k, NH : NH + NS, :]).astype(bf16) for k in range(2)]
    for k in range(2):
        edge_out[k] = dot(jnp.exp(wide_dot(row_masks[k], logs[k])).astype(bf16), expand)
    stacked = [part for k in range(2) for part in split(logs[k])] + [steps[k].astype(bf16) for k in range(2)]
    wide = dot(jnp.concatenate(stacked, axis=0), spread[...])
    wide = [wide[i * 128 : (i + 1) * 128] for i in range(6)]
    later, sooner, equal = triangle[0], triangle[1], triangle[2]
    masks = (later.astype(bf16), sooner.astype(bf16))
    time_r, time_c = iotas(TW, TW)
    first, second = ones_where(time_c <= time_r), ones_where(time_c >= time_r)
    walk = jnp.concatenate([first, first, second, second], axis=1)
    allowed = (later + equal, sooner + equal)
    across = []
    for q in range(4):
        rows = slice(q * TW, (q + 1) * TW)
        parts = [wide[i][rows].astype(bf16) * masks[i // 2] for i in range(4)]
        gaps = dot(walk, jnp.concatenate(parts, axis=0))
        weights = jnp.zeros((TW, NH * TW), f32)
        for k, keep in enumerate(allowed):
            scores = dot_t(read[k][rows], jnp.concatenate([write[k][rows]] * NH, axis=0))
            step_row = jnp.sum(wide[4 + k][rows] * equal, axis=0, keepdims=True)
            weights = weights + scores * step_row * keep
        weights = (weights * jnp.exp(gaps)).astype(bf16)
        values = own[rows]
        spread_values = jnp.concatenate(
            [values * heads[h] for h in range(NH)], axis=0
        )
        result = dot(weights, spread_values)
        reads_out[q] = jnp.concatenate([reach[0][rows], reach[1][rows]], axis=0)
        across.append(result)
    across = jnp.concatenate(across, axis=0)

    skips = dot_wide(d_skip[...], expand)
    own_wide = own.astype(f32)
    vertical = (skips[2:3] + skips[3:4]) * own_wide
    for s in range(8):
        factor = dot(vertical_weights, pick[112 - NH * s : 240 - NH * s, :])
        values = strip_mixed[s].astype(f32)
        vertical = vertical + factor * jnp.concatenate([values] * 4, axis=0)
    base_out[...] = across + (skips[0:1] + skips[1:2]) * own_wide + vertical.astype(bf16).astype(f32)


def final(nb, gathered, *refs):
    count = 1 if gathered else nb
    blocks, refs = refs[:count], refs[count:]
    base_in, reads_in, edge_in, gate_in = refs[:4]
    w_in, conv_w, conv_b, w_proj, dt_bias, a_rate, gain, w_out, out = refs[4:13]
    pre, mixed, la_all, dt_all, totals, attended, scaled = refs[13:]
    row, col = lax.axis_index("rows"), lax.axis_index("cols")
    lower = row == 1
    ng = nb // 8
    w_x = w_in[:, :D]

    def pre_conv(tokens):
        return dot(tokens, w_x).astype(bf16).astype(f32)

    pre[:, 0:8, :] = jnp.zeros((5, 8, D), f32)
    pre[:, 8 + nb * TW :, :] = jnp.zeros((5, 8, D), f32)

    def place_block(tokens, position):
        rows = pre_conv(tokens)
        base = pl.multiple_of(position * TW + 8, 8)
        for q in range(5):
            pre[q, pl.ds(base, TW), :] = rows[q * TW : (q + 1) * TW]

    if gathered:
        each(nb, lambda j: place_block(blocks[0][j, 0:160, :], j))
    else:
        for step in range(nb):
            place_block(blocks[step][0:160, :], col ^ step)
    taps, bias = direction_taps(conv_w, lower), conv_b[...]

    head_lane = ones_where(iotas(NH, 128)[1] % NH == iotas(NH, 128)[0])
    tok_r, tok_c = iotas(128, 128)
    same_row = tok_r // TW == tok_c // TW
    after = ones_where(same_row & (tok_c > tok_r))
    before = ones_where(same_row & (tok_c < tok_r))
    row_ones = ones_where(same_row)
    lane = lax.broadcasted_iota(jnp.int32, (1, 128), 1)
    bias_2 = dot_wide(dt_bias[0:2, :], head_lane)
    rate_2 = dot_wide(a_rate[0:2, :], head_lane)

    def first_pass(g):
        group = lane // NH + g * 8
        is_left = group < col
        w_step = jnp.concatenate(
            [jnp.where(g * 8 + j < col, w_proj[0, 0:NH, :], w_proj[1, 0:NH, :]) for j in range(8)], axis=0
        )
        raw = jnp.zeros((128, 128), f32)
        for j in range(8):
            base = g * (8 * TW) + (8 + TW * j)
            for q in range(1, 5):
                mixed[g * 8 + j, (q - 1) * TW : q * TW, :] = filtered(pre, 5, q, base, taps, bias)
            raw = jnp.where(lane // NH == j, dot_t(mixed[g * 8 + j], w_step), raw)
            block = g * 8 + j
            side = lax.broadcasted_iota(jnp.int32, (1, 2 * TW), 1) < TW
            keep = jnp.where(side, jnp.where(block < col, 1.0, 0.0), jnp.where(block > col, 1.0, 0.0))
            for q in range(4):
                tokens = mixed[g * 8 + j, q * TW : (q + 1) * TW, :]
                attended[q, at(g, j), :] = (dot_t(tokens, reads_in[q]) * keep).astype(bf16)
        steps = softplus(raw + jnp.where(is_left, bias_2[0:1], bias_2[1:2]))
        steps = jnp.where(group == col, 0.0, steps)
        logs = -steps * jnp.where(is_left, rate_2[0:1], rate_2[1:2])
        dt_all[g] = steps
        la_all[g] = logs
        totals[g] = wide_dot(row_ones, logs)

    each(ng, first_pass)

    both_ways = jnp.concatenate([after, before], axis=1)

    def second_pass(g):
        group = lane // NH + g * 8
        logs = la_all[g]
        stacked = jnp.concatenate([jnp.where(group < col, logs, 0.0), jnp.where(group > col, logs, 0.0)], axis=0)
        reach = wide_dot(both_ways, stacked)

        def add_group(other, total):
            source, target = other * 8 + tok_r // NH, g * 8 + tok_c // NH
            nearer = ((source > target) & (source < col)) | ((source < target) & (source > col))
            nearer = nearer & (tok_r % NH == tok_c % NH)
            return total + dot_wide(totals[other], ones_where(nearer))

        if ng == 1:
            reach = add_group(0, reach)
        else:
            reach = lax.fori_loop(0, ng, add_group, reach)
        weight = jnp.concatenate(split(jnp.exp(reach) * dt_all[g]), axis=1)
        expand_r, expand_c = iotas(256, D)
        for j in range(8):
            pick = ones_where((expand_r % 128) == j * NH + expand_c // NH)
            factor = dot(weight, pick)
            values = (mixed[g * 8 + j].astype(f32) * factor).astype(bf16)
            for q in range(4):
                scaled[q, at(g, j), :] = values[q * TW : (q + 1) * TW]

    each(ng, second_pass)

    finish(lower, attended, 0, scaled, base_in, gate_in, edge_in, gain, w_out, out)


def finish(lower, attended, axis, scaled, base_in, gate_in, edge_in, gain, w_out, out):
    entered = []
    for q in range(4):
        rows = slice(q * TW, (q + 1) * TW)
        both = lax.dot_general(attended[q], scaled[q], (((axis,), (0,)), ((), ())), preferred_element_type=f32)
        entered.append(both[:TW] * edge_in[0, rows, :] + both[TW:] * edge_in[1, rows, :])
    combined = base_in[...] + jnp.concatenate(entered, axis=0)

    centre = combined - jnp.mean(combined, axis=-1, keepdims=True)
    normed = centre * lax.rsqrt(jnp.mean(centre * centre, axis=-1, keepdims=True) + norm_eps) * gain[...]
    gated = (normed * gate_in[...]).astype(bf16)
    result = dot(gated, w_out[...]).astype(bf16)
    for i in range(4):
        out[jnp.where(lower, i, 3 - i)] = result[i * TW : (i + 1) * TW]


def early(strip_pre, first, second, third, w_in, conv_w, conv_b, pre, mixed, shifted):
    col = lax.axis_index("cols")
    lower = lax.axis_index("rows") == 1
    w_x = w_in[:, :D]
    pre[:, 0:8, :] = jnp.zeros((5, 8, D), f32)
    pre[:, 136:144, :] = jnp.zeros((5, 8, D), f32)
    for step, block in ((1, first), (2, second), (3, third)):
        place_rows(pre, block, w_x, (col & 3) ^ step)
    base = pl.multiple_of((col & 3) * TW + 8, 8)
    for q in range(5):
        pre[q, pl.ds(base, TW), :] = strip_pre[3 + q]
    taps, bias = direction_taps(conv_w, lower), conv_b[...]
    for q in range(1, 5):
        for j, part in enumerate(filter_row(pre, 5, q, 128, shifted.at[q % 2], taps, bias)):
            mixed[q - 1, TW * j : TW * (j + 1), :] = part


def place_rows(pre, block, w_x, position):
    rows = dot(block[0:160, :], w_x).astype(bf16).astype(f32)
    base = pl.multiple_of(position * TW + 8, 8)
    for q in range(5):
        pre[q, pl.ds(base, TW), :] = rows[q * TW : (q + 1) * TW]


def late(*refs):
    blocks, arrived_pre, refs = (refs[0], refs[1], refs[3]), refs[2], refs[4:]
    (half_pre, half_mixed, base_in, reads_in, edge_in, gate_in), refs = refs[:6], refs[6:]
    pick, ordered, nearer, keep, w_step, lanes = refs[:6]
    refs = refs[6:]
    w_in, conv_w, conv_b, _, _, _, gain, w_out, out = refs[:9]
    pre, mixed, attended, scaled, shifted = refs[9:]
    pre[:, 0:8, :] = jnp.zeros((5, 8, D), f32)
    pre[:, 136:144, :] = jnp.zeros((5, 8, D), f32)
    row, col = lax.axis_index("rows"), lax.axis_index("cols")
    lower = row == 1
    on_left = col < 4
    w_x = w_in[:, :D]
    for step, block in zip((0, 1, 3), blocks):
        place_rows(pre, block, w_x, (col & 3) ^ step)
    base = pl.multiple_of(((col & 3) ^ 2) * TW + 8, 8)
    for q in range(5):
        pre[q, pl.ds(base, TW), :] = arrived_pre[0, q]
    zero = jnp.zeros((1, D), f32)
    for q in range(5):
        pre[q, 7:8, :] = jnp.where(on_left, half_pre[q, 135:136, :], zero)
        pre[q, 136:137, :] = jnp.where(on_left, zero, half_pre[q, 8:9, :])
    taps, bias = direction_taps(conv_w, lower), conv_b[...]
    for q in range(4):
        for j, part in enumerate(filter_row(pre, 5, q + 1, 128, shifted.at[q % 2], taps, bias)):
            mixed[q, 128 + TW * j : 128 + TW * (j + 1), :] = part
    tile = lax.broadcasted_iota(jnp.int32, (16, D), 0)
    low_place, high_place = jnp.where(on_left, 16, 0), jnp.where(on_left, 15, 16)
    for q in range(4):
        total = bias
        for a in range(3):
            if q + a < 5:
                at_left = (half_pre[q + a, 134:135, :], half_pre[q + a, 135:136, :], pre[q + a, 8:9, :])
                at_right = (pre[q + a, 135:136, :], half_pre[q + a, 8:9, :], half_pre[q + a, 9:10, :])
                for b in range(3):
                    total = total + taps[a][b] * jnp.where(on_left, at_left[b], at_right[b])
        value = silu(total)
        mixed[q, 16:112, :] = half_mixed[q, 16:112, :]
        for start, place in ((0, low_place), (112, high_place)):
            held = half_mixed[q, start : start + 16, :].astype(f32)
            mixed[q, start : start + 16, :] = jnp.where(tile == place, value, held).astype(bf16)

    lane = lax.broadcasted_iota(jnp.int32, (1, 128), 1)
    raw = []
    for q in range(4):
        result = dot_t(mixed[q], w_step[...])
        row_raw = result[0:TW]
        for j in range(1, 8):
            row_raw = jnp.where(lane // NH == j, result[TW * j : TW * (j + 1)], row_raw)
        raw.append(row_raw)
        attended[q] = (dot_t(reads_in[q], mixed[q]) * keep[...]).astype(bf16)
    raw = jnp.concatenate(raw, axis=0)
    left, right = lanes[2:3, :], lanes[3:4, :]
    steps = softplus(raw + lanes[0:1, :]) * (left + right)
    logs = -steps * lanes[1:2, :]
    stacked = jnp.concatenate([logs * left, logs * right, dot_wide(logs, nearer[...])], axis=0)
    reach = wide_dot(ordered[...], stacked)
    weight = split(jnp.exp(reach) * steps)
    for j in range(8):
        mask = pick[112 - NH * j : 240 - NH * j, :]
        factor = dot(weight[0], mask).astype(bf16)
        for q in range(4):
            cells = slice(TW * j, TW * (j + 1))
            scaled[q, cells, :] = mixed[q, cells, :] * factor[q * TW : (q + 1) * TW]
    finish(lower, attended, 1, scaled, base_in, gate_in, edge_in, gain, w_out, out)


def shards(feats, w_in, conv_w, conv_b, w_proj, dt_bias, a_rate, d_skip, norm_gain, w_out):
    nb = lax.axis_size("cols")
    direct = nb == 8
    vmem, hbm = pl.BlockSpec(memory_space=pltpu.VMEM), pl.BlockSpec(memory_space=pltpu.HBM)

    def shape(*dims, dtype=f32):
        return jax.ShapeDtypeStruct(dims, dtype)

    def limit(mib):
        return pltpu.CompilerParams(vmem_limit_bytes=mib << 20)

    partner = lax.ppermute(feats, "rows", [(0, 1), (1, 0)])
    params = [w_in, conv_w, conv_b[None], jnp.swapaxes(w_proj, 1, 2), dt_bias, a_rate, d_skip, norm_gain[None], w_out]
    loaded = pl.pallas_call(
        load,
        out_shape=shape(HALO, D, dtype=bf16),
        in_specs=[hbm],
        out_specs=vmem,
        scratch_shapes=[pltpu.SemaphoreType.DMA((4,))],
        compiler_params=limit(8),
    )(pltpu.with_memory_space_constraint(feats, pltpu.HBM))
    params = pl.pallas_call(
        load_weights,
        out_shape=tuple(shape(*part.shape, dtype=part.dtype) for part in params),
        in_specs=[hbm] * 9,
        out_specs=(vmem,) * 9,
        scratch_shapes=[pltpu.SemaphoreType.DMA((9,))],
        compiler_params=limit(8),
    )(*[pltpu.with_memory_space_constraint(part, pltpu.HBM) for part in params])
    w_in, conv_w, conv_b, w_proj, dt_bias, a_rate, d_skip, norm_gain, w_out = params
    sent, short, far = pl.pallas_call(
        pack,
        out_shape=tuple(shape(count, D, dtype=bf16) for count in (HALO, 160, 96)),
        in_specs=[vmem] * 2,
        out_specs=(vmem,) * 3,
        input_output_aliases={0: 0},
        compiler_params=limit(4),
    )(loaded, partner)
    if direct:

        def across(part, step):
            return lax.ppermute(part, "cols", [(i, i ^ step) for i in range(nb)])

        blocks = [sent] + [None] * 7
        for block in START_ORDER:
            source = FORWARDED.get(block)
            own = short if block in (2, 4) else sent
            blocks[block] = across(own, block) if source is None else across(blocks[source], block ^ source)
        sides = [blocks[1], blocks[3], blocks[7]]
    else:
        blocks = sides = [lax.all_gather(sent, "cols")]
    outs = [
        shape(8, TW, D),
        shape(128, D),
        shape(3, TW, NH * TW),
        shape(NH, NH * TW, dtype=bf16),
        shape(NH, TW, D, dtype=bf16),
        shape(256, 128, dtype=bf16),
        shape(128, 256),
        shape(128, 512, dtype=bf16),
        shape(128, 512, dtype=bf16),
        shape(2, 128, 128, dtype=bf16),
        shape(240, D, dtype=bf16),
    ]
    if direct:
        outs += [
            shape(128, 384, dtype=bf16),
            shape(128, 128, dtype=bf16),
            shape(2 * TW, 256),
            shape(128, D, dtype=bf16),
            shape(8, 128),
            shape(1, 5, TW, D),
        ]
    strip_pre, gate, *masks = pl.pallas_call(
        functools.partial(ahead, nb),
        out_shape=tuple(outs),
        in_specs=[vmem] * (7 if direct else 6),
        out_specs=(vmem,) * len(outs),
        compiler_params=limit(8),
        cost_estimate=pl.CostEstimate(flops=200_000_000, bytes_accessed=1_500_000, transcendentals=50_000),
    )(sent, far, w_in, w_proj, dt_bias, a_rate, *((blocks[6],) if direct else ()))
    kept = pl.pallas_call(
        functools.partial(local, nb, len(sides)),
        out_shape=(shape(128, D), shape(4, 2 * TW, D, dtype=bf16), shape(2, 128, D)),
        in_specs=[vmem] * (17 + len(sides)),
        out_specs=(vmem,) * 3,
        scratch_shapes=[pltpu.VMEM((8, 48, D), f32), pltpu.VMEM((2, 2, 48, D), f32)],
        compiler_params=limit(16 if direct else 32),
        cost_estimate=pl.CostEstimate(flops=1_000_000_000, bytes_accessed=4_000_000, transcendentals=1_000_000),
    )(*sides, w_in, conv_w, conv_b, w_proj, dt_bias, a_rate, d_skip, strip_pre, *masks[:9])
    kept = [*kept, gate]
    tail = [w_in, conv_w, conv_b, w_proj, dt_bias, a_rate, norm_gain, w_out]
    if direct:
        half = pl.pallas_call(
            early,
            out_shape=(shape(5, 144, D), shape(4, 128, D, dtype=bf16)),
            in_specs=[vmem] * 7,
            out_specs=(vmem,) * 2,
            scratch_shapes=[pltpu.VMEM((2, 2, 144, D), f32)],
            compiler_params=limit(8),
            cost_estimate=pl.CostEstimate(flops=200_000_000, bytes_accessed=1_500_000, transcendentals=200_000),
        )(strip_pre, *blocks[1:4], w_in, conv_w, conv_b)
        operands = [*blocks[4:6], masks[-1], blocks[7], *half, *kept, *masks[8:-1], *tail]
        body = late
        scratch = [
            pltpu.VMEM((5, 144, D), f32),
            pltpu.VMEM((4, 256, D), bf16),
            pltpu.VMEM((4, 2 * TW, 256), bf16),
            pltpu.VMEM((4, 256, D), bf16),
            pltpu.VMEM((2, 2, 144, D), f32),
        ]
    else:
        operands = [*blocks, *kept, *tail]
        body = functools.partial(final, nb, True)
        scratch = [
            pltpu.VMEM((5, nb * TW + 16, D), f32),
            pltpu.VMEM((nb, 128, D), bf16),
            pltpu.VMEM((nb // 8, 128, 128), f32),
            pltpu.VMEM((nb // 8, 128, 128), f32),
            pltpu.VMEM((nb // 8, 128, 128), f32),
            pltpu.VMEM((4, nb * TW, 2 * TW), bf16),
            pltpu.VMEM((4, nb * TW, D), bf16),
        ]
    return pl.pallas_call(
        body,
        out_shape=shape(TH, TW, D, dtype=bf16),
        in_specs=[vmem] * len(operands),
        out_specs=vmem,
        scratch_shapes=scratch,
        compiler_params=limit(16 if direct else 48),
        cost_estimate=pl.CostEstimate(flops=1_000_000_000, bytes_accessed=4_000_000, transcendentals=1_000_000),
    )(*operands)


def solution(mesh):
    in_specs = (P(("groups", "rows"), "cols", None), P(), P(), P(), P(), P(), P(), P(), P(), P())
    out_specs = P(("groups", "rows"), "cols", None)
    return jax.shard_map(shards, mesh=mesh, in_specs=in_specs, out_specs=out_specs, check_vma=False)
```
